32 devices in a mesh: gx: 4 (over x, core), gy: 2 (over y), gz: 4 (over z).
Axes of the slice: x: 2, y: 2, z: 4, core: 2. Of those that a mesh axis runs over, the one named last changes fastest.
Arguments:
- state: float32 [24, 32, 16, 512], P(None, 'gx', 'gy', 'gz'), may hold values from -6 to 6
- coarse_bricks: float32 [4, 2, 4, 235008], P('gx', 'gy', 'gz'), may hold values from -6 to 6
- shifts: int32 [2], replicated, may hold values from 1 to 8, as said below
- brick_owner: int32 [4], replicated, may hold values from 0 to 3, each once
Outputs:
- new_state: float32 [24, 32, 16, 512], P(None, 'gx', 'gy', 'gz')
The draws below stay inside these ranges and needn't reach their ends.
Inputs may be any that keep to these rules, and one draw needn't show every extreme that they name: shifts[0] and shifts[1] are each from 1 to 8, and at least one of them equals 8. `brick_owner`: a permutation of the gx indices.
All inputs are finite; a program needn't handle non-finite values.
Results may differ from the reference program's by a relative error of at most 0.000062.
Values sent between devices are 32-bit elements; how exact they have to be, the bound alone decides.
A program may use at most 128 MiB of HBM per device.

```python
import jax
import jax.numpy as jnp
from jax import lax

FIELDS = 24
CXY = 8
CZ = 128
BXY = 12
BZ = 68
NX = 32
NY = 16
NZ = 512
N_GX = 4
N_GY = 2
N_GZ = 4


def draw_shifts(key, part):
    key_other = jax.random.fold_in(key, 11)
    key_which = jax.random.fold_in(key, 23)
    other = jax.random.randint(key_other, (), 1, CXY + 1)
    which = jax.random.randint(key_which, (), 0, 2)
    return jnp.where(jnp.arange(2) == which, CXY, other).astype(jnp.int32)


def level_of(key, shape, split, least, high):
    gain = 1.0
    for position, blocks in split:
        steps = jax.random.uniform(jax.random.fold_in(jax.random.fold_in(key, 6), position), (blocks,), jnp.float32, least / len(split), high / len(split))
        gain = gain * jnp.repeat(jnp.exp(steps), shape[position] // blocks).reshape((-1,) + (1,) * (len(shape) - 1 - position))
    return gain


def centred(stream_key, extent, scale, bound, split=(), kind=jnp.bfloat16):
    values = jax.random.normal(stream_key, extent, jnp.float32) * scale
    if len(split) > 0:
        values = level_of(stream_key, extent, split, -0.22, 0.18) * values
    return jnp.clip(values, min=-bound, max=bound).astype(kind)


def setup_inputs(seed: int = 0) -> dict:
    key_list = jax.random.split(jax.random.key(seed), 5)
    state = centred(key_list[0], (FIELDS, NX, NY, NZ), 1.0, 6.0, ((1, 4), (2, 2), (3, 4)), jnp.float32)
    coarse_bricks = centred(key_list[1], (N_GX, N_GY, N_GZ, FIELDS * BXY * BXY * BZ), 1.0, 6.0, ((0, 4), (1, 2), (2, 4)), jnp.float32)
    shifts = draw_shifts(jax.random.fold_in(key_list[4], 71), 0)
    brick_owner = jax.random.permutation(key_list[3], N_GX).astype(jnp.int32)
    return {"state": state, "coarse_bricks": coarse_bricks, "shifts": shifts, "brick_owner": brick_owner}


EVEN_W = (-0.0390625, 0.2734375, 0.8203125, -0.0546875)
ODD_W = (-0.0546875, 0.8203125, 0.2734375, -0.0390625)
PAIRS = ((0, 0), (0, 1), (0, 2), (1, 1), (1, 2), (2, 2))
SIGMA = 0.3
DRIVER_DAMP = 2.0
STEP = 0.25
HIGH = lax.Precision.HIGHEST


def offset_at(axis_pos, amount):
    return tuple(amount if d == axis_pos else 0 for d in range(3))


def window_cut(padded, margins, offsets, extend):
    starts = [0]
    limits = [padded.shape[0]]
    for d in range(3):
        opening = margins[d] + offsets[d] - extend[d]
        starts.append(opening)
        limits.append(opening + padded.shape[d + 1] - 2 * margins[d] + 2 * extend[d])
    return lax.slice(padded, starts, limits)


def deriv_one(padded, margins, axis_pos, extend=(0, 0, 0)):
    def shifted(amount):
        return window_cut(padded, margins, offset_at(axis_pos, amount), extend)
    return (shifted(-2) - 8.0 * shifted(-1) + 8.0 * shifted(1) - shifted(2)) / 12.0


def deriv_two(padded, margins, axis_pos):
    def shifted(amount):
        return window_cut(padded, margins, offset_at(axis_pos, amount), (0, 0, 0))
    return (-shifted(-2) + 16.0 * shifted(-1) - 30.0 * shifted(0) + 16.0 * shifted(1) - shifted(2)) / 12.0


def dissipate(padded, margins, axis_pos):
    def shifted(amount):
        return window_cut(padded, margins, offset_at(axis_pos, amount), (0, 0, 0))
    return (shifted(-3) - 6.0 * shifted(-2) + 15.0 * shifted(-1) - 20.0 * shifted(0)
            + 15.0 * shifted(1) - 6.0 * shifted(2) + shifted(3)) / 64.0


def corner_mixed(padded):
    def mixed_part(index, outer, inner):
        inner_slope = deriv_one(padded[index:index + 1], (3, 3, 3), inner, offset_at(outer, 2))
        return deriv_one(inner_slope, offset_at(outer, 2), outer)[0]
    return mixed_part


def field_rates(padded, mixed_part):
    margins = (3, 3, 3)

    def grads(lower, upper, axis_pos):
        return deriv_one(padded[lower:upper], margins, axis_pos)

    def curves(lower, upper, axis_pos):
        return deriv_two(padded[lower:upper], margins, axis_pos)

    centre = window_cut(padded, margins, (0, 0, 0), (0, 0, 0))
    curv = centre[7]
    trace_free = centre[8:14]
    driver = centre[21:24]
    shift_grad = [grads(18, 21, d) for d in range(3)]
    spread = shift_grad[0][0] + shift_grad[1][1] + shift_grad[2][2]
    curv_grad = [grads(7, 8, d)[0] for d in range(3)]
    gamma_grad = [grads(14, 17, d) for d in range(3)]
    metric_curves = [curves(1, 7, d) for d in range(3)]
    metric_lap = metric_curves[0] + metric_curves[1] + metric_curves[2]
    lapse_curves = [curves(17, 18, d)[0] for d in range(3)]
    conf_curves = [curves(0, 1, d)[0] for d in range(3)]
    shift_curves = [curves(18, 21, d) for d in range(3)]

    def hessian(index, diagonal, i, j):
        if i == j:
            return diagonal[i]
        return mixed_part(index, min(i, j), max(i, j))

    conf_rate = (spread - curv) / 6.0
    metric_rates = []
    ricci = []
    for s, (i, j) in enumerate(PAIRS):
        value = -2.0 * trace_free[s] + shift_grad[i][j] + shift_grad[j][i]
        if i == j:
            value = value - (2.0 / 3.0) * spread
        metric_rates.append(value)
        ricci.append(-hessian(17, lapse_curves, i, j) - 2.0 * hessian(0, conf_curves, i, j)
                     - 0.5 * metric_lap[s] + 0.5 * (gamma_grad[i][j] + gamma_grad[j][i]))
    curv_rate = -(lapse_curves[0] + lapse_curves[1] + lapse_curves[2])
    ricci_trace = ricci[0] + ricci[3] + ricci[5]
    free_rates = []
    for s, (i, j) in enumerate(PAIRS):
        free_rates.append(ricci[s] - ricci_trace / 3.0 if i == j else ricci[s])
    gamma_rates = []
    for i in range(3):
        spread_grad = shift_curves[i][i]
        for k in range(3):
            if k != i:
                spread_grad = spread_grad + mixed_part(18 + k, i, k)
        lap_shift = shift_curves[0][i] + shift_curves[1][i] + shift_curves[2][i]
        gamma_rates.append(-(4.0 / 3.0) * curv_grad[i] + lap_shift + spread_grad / 3.0)
    lapse_rate = -2.0 * curv
    shift_rates = [0.75 * driver[i] for i in range(3)]
    driver_rates = [gamma_rates[i] - DRIVER_DAMP * driver[i] for i in range(3)]
    rates = jnp.stack([conf_rate] + metric_rates + [curv_rate] + free_rates + gamma_rates
                      + [lapse_rate] + shift_rates + driver_rates)
    damping = dissipate(padded, margins, 0) + dissipate(padded, margins, 1) + dissipate(padded, margins, 2)
    return rates + SIGMA * damping


def advance(start, section_rates):
    rate_one = section_rates(start)
    rate_two = section_rates(start + (0.5 * STEP) * rate_one)
    rate_three = section_rates(start + (0.5 * STEP) * rate_two)
    rate_four = section_rates(start + STEP * rate_three)
    return start + (STEP / 6.0) * (rate_one + 2.0 * rate_two + 2.0 * rate_three + rate_four)


def lagrange(shift, rows, cols):
    spots = jnp.arange(rows, dtype=jnp.int32) + shift
    first_col = spots // 2 + spots % 2
    odd_spot = (spots % 2) == 1
    columns = jnp.arange(cols, dtype=jnp.int32)
    matrix = jnp.zeros((rows, cols), jnp.float32)
    for t in range(4):
        weight = jnp.where(odd_spot, ODD_W[t], EVEN_W[t])
        matrix = matrix + jnp.where(columns[None, :] == (first_col + t)[:, None], weight[:, None], 0.0)
    return matrix


def reference(state, coarse_bricks, shifts, brick_owner):
    fields, size_x, size_y, size_z = state.shape
    shift_x = shifts[0].astype(jnp.int32)
    shift_y = shifts[1].astype(jnp.int32)
    zero_index = jnp.zeros((), jnp.int32)
    widened = jnp.pad(state, ((0, 0), (0, CXY), (0, CXY), (0, 0)))
    moved = lax.dynamic_slice(widened, (zero_index, shift_x, shift_y, zero_index), state.shape)
    along_x = lagrange(shift_x, CXY, BXY)
    along_y = lagrange(shift_y, CXY, BXY)
    along_z = lagrange(zero_index, CZ, BZ)
    ordered = jnp.take(coarse_bricks, brick_owner, axis=0)
    ordered = ordered.reshape((N_GX, N_GY, N_GZ, FIELDS, BXY, BXY, BZ))

    def one_row(bricks):
        first_pass = jnp.einsum("bcfpqr,kr->bcfpqk", bricks, along_z, precision=HIGH)
        second_pass = jnp.einsum("bcfpqk,jq->bcfpjk", first_pass, along_y, precision=HIGH)
        return jnp.einsum("bcfpjk,ip->bcfijk", second_pass, along_x, precision=HIGH)

    refill = lax.map(one_row, ordered)
    refill = jnp.transpose(refill, (3, 0, 4, 1, 5, 2, 6)).reshape(state.shape)
    rows = jnp.arange(size_x, dtype=jnp.int32)
    cols = jnp.arange(size_y, dtype=jnp.int32)
    entering = (rows + shift_x >= size_x)[:, None] | (cols + shift_y >= size_y)[None, :]
    start = jnp.where(entering[None, :, :, None], refill, moved)

    def section_rates(values):
        padded = jnp.pad(values, ((0, 0), (3, 3), (3, 3), (3, 3)))
        return field_rates(padded, corner_mixed(padded))

    return advance(start, section_rates)
```

```python
import jax
import jax.numpy as jnp
from jax import lax
from jax.experimental import pallas as pl
from jax.experimental.pallas import tpu as pltpu
from jax.sharding import PartitionSpec as P

EVEN_W = (-0.0390625, 0.2734375, 0.8203125, -0.0546875)
ODD_W = (-0.0546875, 0.8203125, 0.2734375, -0.0390625)
PAIRS = ((0, 0), (0, 1), (0, 2), (1, 1), (1, 2), (2, 2))
SIGMA = 0.3
DRIVER_DAMP = 2.0
STEP = 0.25
HIGH = lax.Precision.HIGHEST


def passed_along(block, axis, distance):
    devices = range(lax.axis_size(axis))
    route = [(i - distance, i) for i in devices if i - distance in devices]
    return lax.ppermute(block, axis, route)


MESH = pl.DeviceIdType.MESH
ORDER = (0, 17, 18, 19, 20, 1, 2, 3, 4, 5, 6, 7, 8, 9, 10, 11, 12, 13, 14, 15, 16, 21, 22, 23)
PLACE = {field: place for place, field in enumerate(ORDER)}
MIXED = 5
FACES = tuple(
    tuple(side if d == axis else 0 for d in range(3)) for axis in range(3) for side in (-1, 1)
)
EDGES = tuple(
    (dx, dy, dz)
    for dx in (-1, 0, 1)
    for dy in (-1, 0, 1)
    for dz in (-1, 0, 1)
    if abs(dx) + abs(dy) + abs(dz) == 2
)
ROUTES = FACES + EDGES


def slope(m2, m1, p1, p2):
    return (8.0 * (p1 - m1) - (p2 - m2)) * (1.0 / 12.0)


def step_kernel(
    start_ref, out_ref, box, zhalo, acc, slopes, ysend, yrecv, csend, crecv, zsend, zcore, zx, zy,
    send_sem, recv_sem,
):
    fields = start_ref.shape[0]
    groups = zsend.shape[2]
    counts = tuple(lax.axis_size(name) for name in ("gx", "gy", "gz"))
    place = tuple(lax.axis_index(name) for name in ("gx", "gy", "gz"))
    lane = lax.broadcasted_iota(jnp.int32, (8, 128), 1)
    row = lax.broadcasted_iota(jnp.int32, (8, 128), 0)
    zero = jnp.zeros((8, 128), jnp.float32)

    def present(route):
        ok = None
        for d in range(3):
            if route[d] != 0:
                here = place[d] > 0 if route[d] < 0 else place[d] < counts[d] - 1
                ok = here if ok is None else jnp.logical_and(ok, here)
        return ok

    def peer(route):
        return tuple(place[d] + route[d] for d in range(3))

    def opposite(route):
        return tuple(-side for side in route)

    def wipe_field(f, carry):
        for slot in range(2):
            for x in range(14):
                for y in (0, 16) if 3 <= x < 11 else (0, 8, 16):
                    box[slot, f, x, pl.ds(y, 8), :] = zero
        for x in range(8):
            value = start_ref[f, x]
            acc[f, x] = value
        return carry

    lax.fori_loop(0, fields, wipe_field, 0)
    for f in range(fields):
        for x in range(8):
            box[0, f, 3 + x, pl.ds(8, 8), :] = start_ref[ORDER[f], x]
    for slot in range(2):
        for z in range(2):
            for g in range(groups):
                zcore[slot, z, g] = zero
            for side in range(2):
                for g in range(2):
                    zx[slot, side, z, g] = zero
                    zy[slot, side, z, g] = zero
            for side in range(2):
                for f in range(MIXED):
                    crecv[slot, z, side, f] = zero

    def wipe_y(f, carry):
        for slot in range(2):
            for side in range(2):
                for j in range(3):
                    yrecv[slot, side, j, f] = zero
        return carry

    lax.fori_loop(0, fields, wipe_y, 0)

    barrier = pltpu.get_barrier_semaphore()
    total = jnp.int32(0)
    for route in ROUTES:
        ok = present(route)
        total = total + ok.astype(jnp.int32)

        @pl.when(ok)
        def _(route=route):
            pl.semaphore_signal(barrier, inc=1, device_id=peer(route), device_id_type=MESH)

    pl.semaphore_wait(barrier, total)

    def message(number, slot):
        route = ROUTES[number]
        dx, dy, dz = route
        low = lambda side: 1 if side < 0 else 0
        high = lambda side: 0 if side < 0 else 1
        if dx != 0 and dy == 0 and dz == 0:
            source = box.at[slot, :, pl.ds(3 if dx < 0 else 8, 3), pl.ds(8, 8), :]
            target = box.at[slot, :, pl.ds(11 if dx < 0 else 0, 3), pl.ds(8, 8), :]
        elif dy != 0 and dx == 0 and dz == 0:
            source = ysend.at[slot, high(dy)]
            target = yrecv.at[slot, low(dy)]
        elif dz != 0 and dx == 0 and dy == 0:
            source = zsend.at[slot, high(dz)]
            target = zcore.at[slot, low(dz)]
        elif dz == 0:
            source = csend.at[slot, high(dy)]
            target = crecv.at[slot, low(dy), low(dx)]
        elif dy == 0:
            source = zsend.at[slot, high(dz), pl.ds(0, 2)]
            target = zx.at[slot, low(dx), low(dz)]
        else:
            source = zsend.at[slot, high(dz), pl.ds(0, 2)]
            target = zy.at[slot, low(dy), low(dz)]
        return pltpu.make_async_remote_copy(
            src_ref=source,
            dst_ref=target,
            send_sem=send_sem.at[number],
            recv_sem=recv_sem.at[slot, number],
            device_id=peer(route),
            device_id_type=MESH,
        )

    def launch(slot, wanted):
        for number, route in enumerate(ROUTES):
            if wanted(route):

                @pl.when(present(route))
                def _(number=number):
                    message(number, slot).start()

    def unpacked(from_low, from_high, t):
        return jnp.where(
            lane < 64,
            pltpu.roll(from_high, (128 - 4 * t) % 128, axis=1),
            pltpu.roll(from_low, (124 - 4 * t) % 128, axis=1),
        )

    def stage(s, carry):
        slot = lax.rem(s, 2)
        launch(slot, lambda r: r[1] == 0 and r[2] == 0)

        def pack_y(f, c):
            for j in range(3):
                ysend[slot, 0, j, f] = box[slot, f, pl.ds(3, 8), 8 + j, :]
                ysend[slot, 1, j, f] = box[slot, f, pl.ds(3, 8), 13 + j, :]
            return c

        lax.fori_loop(0, fields, pack_y, 0)
        launch(slot, lambda r: r[0] == 0 and r[2] == 0)
        outer = jnp.logical_or(row < 2, row >= 6)
        for side in range(2):
            for f in range(MIXED):
                csend[slot, side, f] = jnp.where(
                    outer,
                    ysend[slot, side, side, f],
                    pltpu.roll(ysend[slot, side, side + 1, f], 4, axis=0),
                )
        launch(slot, lambda r: r[2] == 0 and r[0] != 0 and r[1] != 0)

        def pack_z(g, c):
            low = zero
            high = zero
            for q in range(4):
                for x in range(8):
                    t = q * 8 + x
                    value = box[slot, 4 * g + q, 3 + x, pl.ds(8, 8), :]
                    inside = jnp.logical_and(lane >= 4 * t, lane < 4 * t + 4)
                    low = jnp.where(inside, pltpu.roll(value, 4 * t, axis=1), low)
                    high = jnp.where(inside, pltpu.roll(value, (4 * t + 4) % 128, axis=1), high)
            zsend[slot, 0, g] = low
            zsend[slot, 1, g] = high
            return c

        lax.fori_loop(0, groups, pack_z, 0)
        launch(slot, lambda r: r[2] != 0)

        for number, route in enumerate(ROUTES):

            @pl.when(present(opposite(route)))
            def _(number=number):
                message(number, slot).wait_recv()

        def spread_y(f, c):
            for j in range(3):
                box[slot, f, pl.ds(3, 8), 5 + j, :] = yrecv[slot, 0, j, f]
                box[slot, f, pl.ds(3, 8), 16 + j, :] = yrecv[slot, 1, j, f]
            return c

        lax.fori_loop(0, fields, spread_y, 0)
        for f in range(MIXED):
            for side, first_row in ((0, 6), (1, 16)):
                for j in range(2):
                    box[slot, f, pl.ds(1, 2), first_row + j, :] = crecv[
                        slot, side, 0, f, pl.ds(6 if j == 0 else 2, 2), :
                    ]
                    box[slot, f, pl.ds(11, 2), first_row + j, :] = crecv[
                        slot, side, 1, f, pl.ds(0 if j == 0 else 4, 2), :
                    ]

        def spread_z(g, c):
            from_low = zcore[slot, 0, g]
            from_high = zcore[slot, 1, g]
            for q in range(4):
                for x in range(8):
                    zhalo[4 * g + q, 2 + x, pl.ds(8, 8), :] = unpacked(
                        from_low, from_high, q * 8 + x
                    )
            return c

        lax.fori_loop(0, groups, spread_z, 0)
        for f in range(MIXED):
            g, q = f // 4, f % 4
            for side in range(2):
                low_x, high_x = zx[slot, side, 0, g], zx[slot, side, 1, g]
                for k in range(2):
                    x = 6 + k if side == 0 else k
                    at = k if side == 0 else 10 + k
                    zhalo[f, at, pl.ds(8, 8), :] = unpacked(low_x, high_x, q * 8 + x)
                low_y, high_y = zy[slot, side, 0, g], zy[slot, side, 1, g]
                for x in range(8):
                    zhalo[f, 2 + x, pl.ds(16 * side, 8), :] = unpacked(low_y, high_y, q * 8 + x)

        share = jnp.where(jnp.logical_or(s == 0, s == 3), STEP / 6.0, STEP / 3.0)
        share = share.astype(jnp.float32)
        reach = jnp.where(s == 2, STEP, 0.5 * STEP).astype(jnp.float32)
        later = 1 - slot

        def slab(x, c):
            def at_z(value, halo, amount):
                if amount > 0:
                    return pltpu.roll(jnp.where(lane < amount, halo, value), 128 - amount, axis=1)
                return pltpu.roll(
                    jnp.where(lane >= 128 + amount, halo, value), -amount, axis=1
                )

            def tile(f, dx=0, dy=0):
                return box[slot, f, 3 + x + dx, pl.ds(8 + dy, 8), :]

            def slope_z(value, halo):
                return slope(*(at_z(value, halo, amount) for amount in (-2, -1, 1, 2)))

            def study(name, gradient=False):
                f = PLACE[name]
                centre = tile(f)
                halo = zhalo[f, 2 + x, pl.ds(8, 8), :]
                pairs = []
                grads = []
                for d in range(3):
                    cells = {}
                    for amount in (-3, -2, -1, 1, 2, 3):
                        if d == 0:
                            cells[amount] = tile(f, amount, 0)
                        elif d == 1:
                            cells[amount] = tile(f, 0, amount)
                        else:
                            cells[amount] = at_z(centre, halo, amount)
                    pairs.append([cells[k] + cells[-k] for k in (1, 2, 3)])
                    if gradient:
                        grads.append(slope(cells[-2], cells[-1], cells[1], cells[2]))
                ones, twos, threes = [pairs[0][k] + pairs[1][k] + pairs[2][k] for k in range(3)]
                damp = (threes - 6.0 * twos + 15.0 * ones - 60.0 * centre) * (SIGMA / 64.0)
                lap = (16.0 * ones - twos - 90.0 * centre) * (1.0 / 12.0)
                curves = [
                    (16.0 * pairs[d][0] - pairs[d][1] - 30.0 * centre) * (1.0 / 12.0)
                    for d in range(3)
                ]
                return centre, damp, lap, curves, grads

            def finish(name, rate):
                f = PLACE[name]
                total = acc[name, x] + share * rate
                acc[name, x] = total
                box[later, f, 3 + x, pl.ds(8, 8), :] = start_ref[name, x] + reach * rate

            def across_x(name, y):
                f = PLACE[name]
                return slope(
                    *(box[slot, f, 3 + x + k, pl.ds(y, 8), :] for k in (-2, -1, 1, 2))
                )

            def halo_x(name):
                f = PLACE[name]
                return slope(
                    *(zhalo[f, 2 + x + k, pl.ds(8, 8), :] for k in (-2, -1, 1, 2))
                )

            def along_y(name):
                f = PLACE[name]
                return slope(*(tile(f, 0, k) for k in (-2, -1, 1, 2)))

            def halo_y(name):
                f = PLACE[name]
                return slope(
                    *(zhalo[f, 2 + x, pl.ds(8 + k, 8), :] for k in (-2, -1, 1, 2))
                )

            def mixed_xy(number, value):
                for y in (0, 8, 16):
                    slopes[number, pl.ds(y, 8), :] = value(lambda name: across_x(name, y))
                return slope(*(slopes[number, pl.ds(8 + k, 8), :] for k in (-2, -1, 1, 2)))

            def mixed_xz(value):
                return slope_z(value(lambda name: across_x(name, 8)), value(halo_x))

            def mixed_yz(value):
                return slope_z(value(along_y), value(halo_y))

            both = lambda part: part(17) + 2.0 * part(0)
            only = lambda name: (lambda part: part(name))

            curv, curv_damp, _, _, curv_grad = study(7, True)
            phi, phi_damp, _, phi_curves, _ = study(0)
            lapse, lapse_damp, lapse_lap, lapse_curves, _ = study(17)
            finish(17, lapse_damp - 2.0 * curv)
            finish(7, curv_damp - lapse_lap)
            shift_parts = [study(18 + i, True) for i in range(3)]
            shift_grad = [[shift_parts[j][4][d] for j in range(3)] for d in range(3)]
            spread = shift_grad[0][0] + shift_grad[1][1] + shift_grad[2][2]
            finish(0, phi_damp + (spread - curv) * (1.0 / 6.0))
            crossed = (
                mixed_xy(0, only(19)) + mixed_xz(only(20)),
                mixed_xy(1, only(18)) + mixed_yz(only(20)),
                mixed_xz(only(18)) + mixed_yz(only(19)),
            )
            gamma_grad = []
            gamma_parts = [study(14 + i, True) for i in range(3)]
            gamma_grad = [[gamma_parts[j][4][d] for j in range(3)] for d in range(3)]
            for i in range(3):
                rate = (
                    shift_parts[i][2]
                    - (4.0 / 3.0) * curv_grad[i]
                    + (shift_parts[i][3][i] + crossed[i]) * (1.0 / 3.0)
                )
                finish(14 + i, rate + gamma_parts[i][1])
                driver, driver_damp, _, _, _ = study(21 + i)
                finish(18 + i, shift_parts[i][1] + 0.75 * driver)
                finish(21 + i, driver_damp + rate - DRIVER_DAMP * driver)
            hessian = {
                (0, 1): mixed_xy(2, both),
                (0, 2): mixed_xz(both),
                (1, 2): mixed_yz(both),
            }
            for i in range(3):
                hessian[(i, i)] = lapse_curves[i] + 2.0 * phi_curves[i]
            ricci = []
            free_damp = []
            for n, (i, j) in enumerate(PAIRS):
                free, damp, _, _, _ = study(8 + n)
                free_damp.append(damp)
                _, metric_damp, metric_lap, _, _ = study(1 + n)
                value = shift_grad[i][j] + shift_grad[j][i] - 2.0 * free
                if i == j:
                    value = value - (2.0 / 3.0) * spread
                finish(1 + n, value + metric_damp)
                ricci.append(
                    0.5 * (gamma_grad[i][j] + gamma_grad[j][i] - metric_lap) - hessian[(i, j)]
                )
            trace = (ricci[0] + ricci[3] + ricci[5]) * (1.0 / 3.0)
            for n, (i, j) in enumerate(PAIRS):
                value = ricci[n] - trace if i == j else ricci[n]
                finish(8 + n, value + free_damp[n])
            return c

        lax.fori_loop(0, 8, slab, 0)
        for number, route in enumerate(ROUTES):

            @pl.when(present(route))
            def _(number=number):
                message(number, slot).wait_send()

        return carry

    lax.fori_loop(0, 4, stage, 0)

    def hand_out(f, carry):
        for x in range(8):
            out_ref[f, x] = acc[f, x]
        return carry

    lax.fori_loop(0, fields, hand_out, 0)


def advance(start):
    fields, width, height, depth = start.shape
    groups = fields * width // 32
    tall = height + 16

    def buffer(*sizes):
        return pltpu.VMEM(sizes + (depth,), jnp.float32)

    return pl.pallas_call(
        step_kernel,
        out_shape=jax.ShapeDtypeStruct(start.shape, jnp.float32),
        in_specs=[pl.BlockSpec(memory_space=pltpu.VMEM)],
        out_specs=pl.BlockSpec(memory_space=pltpu.VMEM),
        scratch_shapes=[
            buffer(2, fields, width + 6, tall),
            buffer(fields, width + 4, tall),
            buffer(fields, width, height),
            buffer(3, tall),
            buffer(2, 2, 3, fields, width),
            buffer(2, 2, 3, fields, width),
            buffer(2, 2, MIXED, width),
            buffer(2, 2, 2, MIXED, width),
            buffer(2, 2, groups, height),
            buffer(2, 2, groups, height),
            buffer(2, 2, 2, 2, height),
            buffer(2, 2, 2, 2, height),
            pltpu.SemaphoreType.DMA((len(ROUTES),)),
            pltpu.SemaphoreType.DMA((2, len(ROUTES))),
        ],
        compiler_params=pltpu.CompilerParams(
            collective_id=0, has_side_effects=True, vmem_limit_bytes=48 * 1024 * 1024
        ),
    )(start)


def lagrange(shift, rows, cols):
    spots = jnp.arange(rows, dtype=jnp.int32) + shift
    first_col = spots // 2 + spots % 2
    odd_spot = spots % 2 == 1
    columns = jnp.arange(cols, dtype=jnp.int32)
    matrix = jnp.zeros((rows, cols), jnp.float32)
    for t in range(4):
        weight = jnp.where(odd_spot, ODD_W[t], EVEN_W[t])
        matrix = matrix + jnp.where(
            columns[None, :] == (first_col + t)[:, None], weight[:, None], 0.0
        )
    return matrix


def body(state, coarse_bricks, shifts, brick_owner):
    fields, width, height, depth = state.shape
    brick_side = width + 4
    brick_depth = depth // 2 + 4
    shift_x = shifts[0]
    shift_y = shifts[1]
    beyond_x = passed_along(state, "gx", -1)
    moved = lax.dynamic_slice_in_dim(
        jnp.concatenate([state, beyond_x], axis=1), shift_x, width, axis=1
    )
    beyond_y = passed_along(moved, "gy", -1)
    moved = lax.dynamic_slice_in_dim(
        jnp.concatenate([moved, beyond_y], axis=2), shift_y, height, axis=2
    )
    place_x = lax.axis_index("gx")
    place_y = lax.axis_index("gy")
    wanted = jnp.sum(
        jnp.where(jnp.arange(brick_owner.shape[0], dtype=jnp.int32) == place_x, brick_owner, 0)
    )
    piece = lax.all_gather(coarse_bricks, "gx", axis=0, tiled=True)
    chosen = (jnp.arange(piece.shape[0], dtype=jnp.int32) == wanted).astype(jnp.float32)
    flat_brick = jnp.sum(piece[:, 0, 0] * chosen[:, None], axis=0)
    brick = flat_brick.reshape((fields, brick_side, brick_side, brick_depth))
    along_x = lagrange(shift_x, width, brick_side)
    along_y = lagrange(shift_y, height, brick_side)
    along_z = lagrange(jnp.zeros((), jnp.int32), depth, brick_depth)
    first_pass = jnp.einsum("fpqr,kr->fpqk", brick, along_z, precision=HIGH)
    second_pass = jnp.einsum("fpqk,jq->fpjk", first_pass, along_y, precision=HIGH)
    refill = jnp.einsum("fpjk,ip->fijk", second_pass, along_x, precision=HIGH)
    rows = place_x * width + jnp.arange(width, dtype=jnp.int32)
    cols = place_y * height + jnp.arange(height, dtype=jnp.int32)
    entering = (rows + shift_x >= width * lax.axis_size("gx"))[:, None] | (
        cols + shift_y >= height * lax.axis_size("gy")
    )[None, :]
    start = jnp.where(entering[None, :, :, None], refill, moved)
    return advance(start)


def solution(mesh):
    return jax.shard_map(
        body,
        mesh=mesh,
        in_specs=(P(None, "gx", "gy", "gz"), P("gx", "gy", "gz", None), P(), P()),
        out_specs=P(None, "gx", "gy", "gz"),
        check_vma=False,
    )
```

```python
import jax
import jax.numpy as jnp
import numpy as np
from jax import lax
from jax.experimental import pallas as pl
from jax.experimental.pallas import tpu as pltpu
from jax.sharding import PartitionSpec as P

EVEN_W = (-0.0390625, 0.2734375, 0.8203125, -0.0546875)
ODD_W = (-0.0546875, 0.8203125, 0.2734375, -0.0390625)
PAIRS = ((0, 0), (0, 1), (0, 2), (1, 1), (1, 2), (2, 2))
SIGMA = 0.3
DRIVER_DAMP = 2.0
STEP = 0.25
HIGH = lax.Precision.HIGHEST


def passed_along(block, axis, distance):
    devices = range(lax.axis_size(axis))
    route = [(i - distance, i) for i in devices if i - distance in devices]
    return lax.ppermute(block, axis, route)


MESH = pl.DeviceIdType.MESH
ORDER = (0, 17, 18, 19, 20, 1, 2, 3, 4, 5, 6, 7, 8, 9, 10, 11, 12, 13, 14, 15, 16, 21, 22, 23)
PLACE = {field: place for place, field in enumerate(ORDER)}
MIXED = 5
PORTIONS = 6
FACES = tuple(
    tuple(side if d == axis else 0 for d in range(3)) for axis in range(3) for side in (-1, 1)
)
EDGES = tuple(
    (dx, dy, dz)
    for dx in (-1, 0, 1)
    for dy in (-1, 0, 1)
    for dz in (-1, 0, 1)
    if abs(dx) + abs(dy) + abs(dz) == 2
)
ROUTES = FACES + EDGES


def slope(m2, m1, p1, p2):
    return (8.0 * (p1 - m1) - (p2 - m2)) * (1.0 / 12.0)


def step_kernel(
    shifts_ref, source_ref, moved_ref, filled_ref, out_ref, start_ref, gathered, box, zhalo, acc, slopes, ysend, yrecv, csend, crecv, zsend, zcore, zx, zy,
    send_sem, recv_sem, own_send, own_recv, far_send, far_recv, on_send, on_recv,
):
    fields = start_ref.shape[0]
    portion = fields // PORTIONS
    groups = zsend.shape[2]
    counts = tuple(lax.axis_size(name) for name in ("gx", "gy", "gz"))
    place = tuple(lax.axis_index(name) for name in ("gx", "gy", "gz"))
    lane = lax.broadcasted_iota(jnp.int32, (8, 128), 1)
    row = lax.broadcasted_iota(jnp.int32, (8, 128), 0)
    zero = jnp.zeros((8, 128), jnp.float32)

    def present(route):
        ok = None
        for d in range(3):
            if route[d] != 0:
                here = place[d] > 0 if route[d] < 0 else place[d] < counts[d] - 1
                ok = here if ok is None else jnp.logical_and(ok, here)
        return ok

    def peer(route):
        return tuple(place[d] + route[d] for d in range(3))

    def opposite(route):
        return tuple(-side for side in route)

    def wipe_field(f, carry):
        for slot in range(2):
            for x in range(14):
                for y in (0, 16) if 3 <= x < 11 else (0, 8, 16):
                    box[slot, f, x, pl.ds(y, 8), :] = zero
        return carry

    lax.fori_loop(0, fields, wipe_field, 0)

    def keep_own(f, carry):
        for x in range(8):
            gathered[0, f, x] = filled_ref[f, x]
        return carry

    for slot in range(2):
        for z in range(2):
            for g in range(groups):
                zcore[slot, z, g] = zero
            for side in range(2):
                for g in range(2):
                    zx[slot, side, z, g] = zero
                    zy[slot, side, z, g] = zero
            for side in range(2):
                for f in range(MIXED):
                    crecv[slot, z, side, f] = zero

    def wipe_y(f, carry):
        for slot in range(2):
            for side in range(2):
                for j in range(3):
                    yrecv[slot, side, j, f] = zero
        return carry

    lax.fori_loop(0, fields, wipe_y, 0)

    barrier = pltpu.get_barrier_semaphore()
    partner = (place[0] + 1 - 2 * lax.rem(place[0], 2), place[1], place[2])
    across = (lax.rem(place[0] + 2, 4), place[1], place[2])
    total = jnp.int32(2)
    for other in (partner, across):
        pl.semaphore_signal(barrier, inc=1, device_id=other, device_id_type=MESH)
    for route in ROUTES:
        ok = present(route)
        total = total + ok.astype(jnp.int32)

        @pl.when(ok)
        def _(route=route):
            pl.semaphore_signal(barrier, inc=1, device_id=peer(route), device_id_type=MESH)

    pl.semaphore_wait(barrier, total)

    def remote(source, target, sent, got, device):
        return pltpu.make_async_remote_copy(
            src_ref=source,
            dst_ref=target,
            send_sem=sent,
            recv_sem=got,
            device_id=device,
            device_id_type=MESH,
        )

    def far_copy(k):
        part = pl.ds(k * portion, portion)
        return remote(
            filled_ref.at[part], gathered.at[2, part], far_send.at[k], far_recv.at[k], across
        )

    def on_copy(k):
        part = pl.ds(k * portion, portion)
        return remote(
            gathered.at[2, part], gathered.at[3, part], on_send.at[k], on_recv.at[k], partner
        )

    own_copy = remote(filled_ref, gathered.at[1], own_send, own_recv, partner)
    for k in range(PORTIONS):
        far_copy(k).start()
    own_copy.start()
    lax.fori_loop(0, fields, keep_own, 0)
    for k in range(PORTIONS):
        far_copy(k).wait_recv()
        on_copy(k).start()
    own_copy.wait()
    for k in range(PORTIONS):
        on_copy(k).wait()
        far_copy(k).wait_send()
    chosen = source_ref[0]
    row_spot = row + (place[1] * 8 + shifts_ref[1])
    column_entering = row_spot >= 8 * counts[1]
    for f in range(fields):
        for x in range(8):
            x_spot = jnp.zeros((8, 128), jnp.int32) + (place[0] * 8 + x + shifts_ref[0])
            entering = jnp.logical_or(column_entering, x_spot >= 8 * counts[0])
            name = ORDER[f]
            value = jnp.where(entering, gathered[chosen, name, x], moved_ref[name, x])
            start_ref[name, x] = value
            acc[name, x] = value
            box[0, f, 3 + x, pl.ds(8, 8), :] = value

    def message(number, slot):
        route = ROUTES[number]
        dx, dy, dz = route
        low = lambda side: 1 if side < 0 else 0
        high = lambda side: 0 if side < 0 else 1
        if dx != 0 and dy == 0 and dz == 0:
            source = box.at[slot, :, pl.ds(3 if dx < 0 else 8, 3), pl.ds(8, 8), :]
            target = box.at[slot, :, pl.ds(11 if dx < 0 else 0, 3), pl.ds(8, 8), :]
        elif dy != 0 and dx == 0 and dz == 0:
            source = ysend.at[slot, high(dy)]
            target = yrecv.at[slot, low(dy)]
        elif dz != 0 and dx == 0 and dy == 0:
            source = zsend.at[slot, high(dz)]
            target = zcore.at[slot, low(dz)]
        elif dz == 0:
            source = csend.at[slot, high(dy)]
            target = crecv.at[slot, low(dy), low(dx)]
        elif dy == 0:
            source = zsend.at[slot, high(dz), pl.ds(0, 2)]
            target = zx.at[slot, low(dx), low(dz)]
        else:
            source = zsend.at[slot, high(dz), pl.ds(0, 2)]
            target = zy.at[slot, low(dy), low(dz)]
        return pltpu.make_async_remote_copy(
            src_ref=source,
            dst_ref=target,
            send_sem=send_sem.at[number],
            recv_sem=recv_sem.at[slot, number],
            device_id=peer(route),
            device_id_type=MESH,
        )

    def launch(slot, wanted):
        for number, route in enumerate(ROUTES):
            if wanted(route):

                @pl.when(present(route))
                def _(number=number):
                    message(number, slot).start()

    def unpacked(from_low, from_high, t):
        return jnp.where(
            lane < 64,
            pltpu.roll(from_high, (128 - 4 * t) % 128, axis=1),
            pltpu.roll(from_low, (124 - 4 * t) % 128, axis=1),
        )

    def stage(s, carry):
        slot = lax.rem(s, 2)
        launch(slot, lambda r: r[1] == 0 and r[2] == 0)

        def pack_y(f, c):
            for j in range(3):
                ysend[slot, 0, j, f] = box[slot, f, pl.ds(3, 8), 8 + j, :]
                ysend[slot, 1, j, f] = box[slot, f, pl.ds(3, 8), 13 + j, :]
            return c

        lax.fori_loop(0, fields, pack_y, 0)
        launch(slot, lambda r: r[0] == 0 and r[2] == 0)
        outer = jnp.logical_or(row < 2, row >= 6)
        for side in range(2):
            for f in range(MIXED):
                csend[slot, side, f] = jnp.where(
                    outer,
                    ysend[slot, side, side, f],
                    pltpu.roll(ysend[slot, side, side + 1, f], 4, axis=0),
                )
        launch(slot, lambda r: r[2] == 0 and r[0] != 0 and r[1] != 0)

        def pack_z(g, c):
            low = zero
            high = zero
            for q in range(4):
                for x in range(8):
                    t = q * 8 + x
                    value = box[slot, 4 * g + q, 3 + x, pl.ds(8, 8), :]
                    inside = jnp.logical_and(lane >= 4 * t, lane < 4 * t + 4)
                    low = jnp.where(inside, pltpu.roll(value, 4 * t, axis=1), low)
                    high = jnp.where(inside, pltpu.roll(value, (4 * t + 4) % 128, axis=1), high)
            zsend[slot, 0, g] = low
            zsend[slot, 1, g] = high
            return c

        lax.fori_loop(0, groups, pack_z, 0)
        launch(slot, lambda r: r[2] != 0)

        for number, route in enumerate(ROUTES):

            @pl.when(present(opposite(route)))
            def _(number=number):
                message(number, slot).wait_recv()

        def spread_y(f, c):
            for j in range(3):
                box[slot, f, pl.ds(3, 8), 5 + j, :] = yrecv[slot, 0, j, f]
                box[slot, f, pl.ds(3, 8), 16 + j, :] = yrecv[slot, 1, j, f]
            return c

        lax.fori_loop(0, fields, spread_y, 0)
        for f in range(MIXED):
            for side, first_row in ((0, 6), (1, 16)):
                for j in range(2):
                    box[slot, f, pl.ds(1, 2), first_row + j, :] = crecv[
                        slot, side, 0, f, pl.ds(6 if j == 0 else 2, 2), :
                    ]
                    box[slot, f, pl.ds(11, 2), first_row + j, :] = crecv[
                        slot, side, 1, f, pl.ds(0 if j == 0 else 4, 2), :
                    ]

        def spread_z(g, c):
            from_low = zcore[slot, 0, g]
            from_high = zcore[slot, 1, g]
            for q in range(4):
                for x in range(8):
                    zhalo[4 * g + q, 2 + x, pl.ds(8, 8), :] = unpacked(
                        from_low, from_high, q * 8 + x
                    )
            return c

        lax.fori_loop(0, groups, spread_z, 0)
        for f in range(MIXED):
            g, q = f // 4, f % 4
            for side in range(2):
                low_x, high_x = zx[slot, side, 0, g], zx[slot, side, 1, g]
                for k in range(2):
                    x = 6 + k if side == 0 else k
                    at = k if side == 0 else 10 + k
                    zhalo[f, at, pl.ds(8, 8), :] = unpacked(low_x, high_x, q * 8 + x)
                low_y, high_y = zy[slot, side, 0, g], zy[slot, side, 1, g]
                for x in range(8):
                    zhalo[f, 2 + x, pl.ds(16 * side, 8), :] = unpacked(low_y, high_y, q * 8 + x)

        share = jnp.where(jnp.logical_or(s == 0, s == 3), STEP / 6.0, STEP / 3.0)
        share = share.astype(jnp.float32)
        reach = jnp.where(s == 2, STEP, 0.5 * STEP).astype(jnp.float32)
        later = 1 - slot

        def slab(x, c):
            def at_z(value, halo, amount):
                if amount > 0:
                    return pltpu.roll(jnp.where(lane < amount, halo, value), 128 - amount, axis=1)
                return pltpu.roll(
                    jnp.where(lane >= 128 + amount, halo, value), -amount, axis=1
                )

            def tile(f, dx=0, dy=0):
                return box[slot, f, 3 + x + dx, pl.ds(8 + dy, 8), :]

            def slope_z(value, halo):
                return slope(*(at_z(value, halo, amount) for amount in (-2, -1, 1, 2)))

            def study(name, gradient=False):
                f = PLACE[name]
                centre = tile(f)
                halo = zhalo[f, 2 + x, pl.ds(8, 8), :]
                pairs = []
                grads = []
                for d in range(3):
                    cells = {}
                    for amount in (-3, -2, -1, 1, 2, 3):
                        if d == 0:
                            cells[amount] = tile(f, amount, 0)
                        elif d == 1:
                            cells[amount] = tile(f, 0, amount)
                        else:
                            cells[amount] = at_z(centre, halo, amount)
                    pairs.append([cells[k] + cells[-k] for k in (1, 2, 3)])
                    if gradient:
                        grads.append(slope(cells[-2], cells[-1], cells[1], cells[2]))
                ones, twos, threes = [pairs[0][k] + pairs[1][k] + pairs[2][k] for k in range(3)]
                damp = (threes - 6.0 * twos + 15.0 * ones - 60.0 * centre) * (SIGMA / 64.0)
                lap = (16.0 * ones - twos - 90.0 * centre) * (1.0 / 12.0)
                curves = [
                    (16.0 * pairs[d][0] - pairs[d][1] - 30.0 * centre) * (1.0 / 12.0)
                    for d in range(3)
                ]
                return centre, damp, lap, curves, grads

            def finish(name, rate):
                f = PLACE[name]
                total = acc[name, x] + share * rate
                acc[name, x] = total
                box[later, f, 3 + x, pl.ds(8, 8), :] = start_ref[name, x] + reach * rate

            def across_x(name, y):
                f = PLACE[name]
                return slope(
                    *(box[slot, f, 3 + x + k, pl.ds(y, 8), :] for k in (-2, -1, 1, 2))
                )

            def halo_x(name):
                f = PLACE[name]
                return slope(
                    *(zhalo[f, 2 + x + k, pl.ds(8, 8), :] for k in (-2, -1, 1, 2))
                )

            def along_y(name):
                f = PLACE[name]
                return slope(*(tile(f, 0, k) for k in (-2, -1, 1, 2)))

            def halo_y(name):
                f = PLACE[name]
                return slope(
                    *(zhalo[f, 2 + x, pl.ds(8 + k, 8), :] for k in (-2, -1, 1, 2))
                )

            def mixed_xy(number, value):
                for y in (0, 8, 16):
                    slopes[number, pl.ds(y, 8), :] = value(lambda name: across_x(name, y))
                return slope(*(slopes[number, pl.ds(8 + k, 8), :] for k in (-2, -1, 1, 2)))

            def mixed_xz(value):
                return slope_z(value(lambda name: across_x(name, 8)), value(halo_x))

            def mixed_yz(value):
                return slope_z(value(along_y), value(halo_y))

            both = lambda part: part(17) + 2.0 * part(0)
            only = lambda name: (lambda part: part(name))

            curv, curv_damp, _, _, curv_grad = study(7, True)
            phi, phi_damp, _, phi_curves, _ = study(0)
            lapse, lapse_damp, lapse_lap, lapse_curves, _ = study(17)
            finish(17, lapse_damp - 2.0 * curv)
            finish(7, curv_damp - lapse_lap)
            shift_parts = [study(18 + i, True) for i in range(3)]
            shift_grad = [[shift_parts[j][4][d] for j in range(3)] for d in range(3)]
            spread = shift_grad[0][0] + shift_grad[1][1] + shift_grad[2][2]
            finish(0, phi_damp + (spread - curv) * (1.0 / 6.0))
            crossed = (
                mixed_xy(0, only(19)) + mixed_xz(only(20)),
                mixed_xy(1, only(18)) + mixed_yz(only(20)),
                mixed_xz(only(18)) + mixed_yz(only(19)),
            )
            gamma_grad = []
            gamma_parts = [study(14 + i, True) for i in range(3)]
            gamma_grad = [[gamma_parts[j][4][d] for j in range(3)] for d in range(3)]
            for i in range(3):
                rate = (
                    shift_parts[i][2]
                    - (4.0 / 3.0) * curv_grad[i]
                    + (shift_parts[i][3][i] + crossed[i]) * (1.0 / 3.0)
                )
                finish(14 + i, rate + gamma_parts[i][1])
                driver, driver_damp, _, _, _ = study(21 + i)
                finish(18 + i, shift_parts[i][1] + 0.75 * driver)
                finish(21 + i, driver_damp + rate - DRIVER_DAMP * driver)
            hessian = {
                (0, 1): mixed_xy(2, both),
                (0, 2): mixed_xz(both),
                (1, 2): mixed_yz(both),
            }
            for i in range(3):
                hessian[(i, i)] = lapse_curves[i] + 2.0 * phi_curves[i]
            ricci = []
            free_damp = []
            for n, (i, j) in enumerate(PAIRS):
                free, damp, _, _, _ = study(8 + n)
                free_damp.append(damp)
                _, metric_damp, metric_lap, _, _ = study(1 + n)
                value = shift_grad[i][j] + shift_grad[j][i] - 2.0 * free
                if i == j:
                    value = value - (2.0 / 3.0) * spread
                finish(1 + n, value + metric_damp)
                ricci.append(
                    0.5 * (gamma_grad[i][j] + gamma_grad[j][i] - metric_lap) - hessian[(i, j)]
                )
            trace = (ricci[0] + ricci[3] + ricci[5]) * (1.0 / 3.0)
            for n, (i, j) in enumerate(PAIRS):
                value = ricci[n] - trace if i == j else ricci[n]
                finish(8 + n, value + free_damp[n])
            return c

        lax.fori_loop(0, 8, slab, 0)
        for number, route in enumerate(ROUTES):

            @pl.when(present(route))
            def _(number=number):
                message(number, slot).wait_send()

        return carry

    lax.fori_loop(0, 4, stage, 0)

    def hand_out(f, carry):
        for x in range(8):
            out_ref[f, x] = acc[f, x]
        return carry

    lax.fori_loop(0, fields, hand_out, 0)


def advance(shifts, source, moved, filled):
    fields, width, height, depth = moved.shape
    groups = fields * width // 32
    tall = height + 16

    def buffer(*sizes):
        return pltpu.VMEM(sizes + (depth,), jnp.float32)

    return pl.pallas_call(
        step_kernel,
        out_shape=jax.ShapeDtypeStruct(moved.shape, jnp.float32),
        in_specs=[pl.BlockSpec(memory_space=pltpu.SMEM)] * 2
        + [pl.BlockSpec(memory_space=pltpu.VMEM)] * 2,
        out_specs=pl.BlockSpec(memory_space=pltpu.VMEM),
        scratch_shapes=[
            buffer(fields, width, height),
            buffer(4, fields, width, height),
            buffer(2, fields, width + 6, tall),
            buffer(fields, width + 4, tall),
            buffer(fields, width, height),
            buffer(3, tall),
            buffer(2, 2, 3, fields, width),
            buffer(2, 2, 3, fields, width),
            buffer(2, 2, MIXED, width),
            buffer(2, 2, 2, MIXED, width),
            buffer(2, 2, groups, height),
            buffer(2, 2, groups, height),
            buffer(2, 2, 2, 2, height),
            buffer(2, 2, 2, 2, height),
            pltpu.SemaphoreType.DMA((len(ROUTES),)),
            pltpu.SemaphoreType.DMA((2, len(ROUTES))),
            pltpu.SemaphoreType.DMA,
            pltpu.SemaphoreType.DMA,
            pltpu.SemaphoreType.DMA((PORTIONS,)),
            pltpu.SemaphoreType.DMA((PORTIONS,)),
            pltpu.SemaphoreType.DMA((PORTIONS,)),
            pltpu.SemaphoreType.DMA((PORTIONS,)),
        ],
        compiler_params=pltpu.CompilerParams(
            collective_id=0, has_side_effects=True, vmem_limit_bytes=48 * 1024 * 1024
        ),
    )(shifts, source, moved, filled)


def lagrange(shift, rows, cols):
    matrix = np.zeros((rows, cols), np.float32)
    for line in range(rows):
        spot = line + shift
        first = spot // 2 + spot % 2
        for t, weight in enumerate(ODD_W if spot % 2 else EVEN_W):
            if first + t < cols:
                matrix[line, first + t] = weight
    return matrix


def lagrange_at(shift, rows, cols):
    table = np.stack([lagrange(s, rows, cols) for s in range(rows + 1)])
    return lax.dynamic_index_in_dim(jnp.asarray(table), shift, 0, keepdims=False)


def body(state, coarse_bricks, shifts, brick_owner):
    fields, width, height, depth = state.shape
    brick_side = width + 4
    brick_depth = depth // 2 + 4
    shift_x = shifts[0]
    shift_y = shifts[1]
    beyond_x = passed_along(state, "gx", -1)
    moved = lax.dynamic_slice_in_dim(
        jnp.concatenate([state, beyond_x], axis=1), shift_x, width, axis=1
    )
    beyond_y = passed_along(moved, "gy", -1)
    moved = lax.dynamic_slice_in_dim(
        jnp.concatenate([moved, beyond_y], axis=2), shift_y, height, axis=2
    )
    place_x = lax.axis_index("gx")
    wanted = jnp.sum(
        jnp.where(jnp.arange(brick_owner.shape[0], dtype=jnp.int32) == place_x, brick_owner, 0)
    )
    brick = coarse_bricks.reshape((fields, brick_side, brick_side, brick_depth))
    along_x = lagrange_at(shift_x, width, brick_side)
    along_y = lagrange_at(shift_y, height, brick_side)
    along_z = jnp.asarray(lagrange(0, depth, brick_depth))
    first_pass = jnp.einsum("fpqr,kr->fpqk", brick, along_z, precision=HIGH)
    second_pass = jnp.einsum("fpqk,jq->fpjk", first_pass, along_y, precision=HIGH)
    filled = jnp.einsum("fpjk,ip->fijk", second_pass, along_x, precision=HIGH)
    source = jnp.bitwise_xor(wanted, place_x).astype(jnp.int32).reshape(1)
    return advance(shifts, source, moved, filled)


def solution(mesh):
    return jax.shard_map(
        body,
        mesh=mesh,
        in_specs=(P(None, "gx", "gy", "gz"), P("gx", "gy", "gz", None), P(), P()),
        out_specs=P(None, "gx", "gy", "gz"),
        check_vma=False,
    )
```

```python
import jax
import jax.numpy as jnp
import numpy as np
from jax import lax
from jax.experimental import pallas as pl
from jax.experimental.pallas import tpu as pltpu
from jax.sharding import PartitionSpec as P

EVEN_W = (-0.0390625, 0.2734375, 0.8203125, -0.0546875)
ODD_W = (-0.0546875, 0.8203125, 0.2734375, -0.0390625)
PAIRS = ((0, 0), (0, 1), (0, 2), (1, 1), (1, 2), (2, 2))
SIGMA = 0.3
DRIVER_DAMP = 2.0
STEP = 0.25
HIGH = lax.Precision.HIGHEST


def passed_along(block, axis, distance):
    devices = range(lax.axis_size(axis))
    route = [(i - distance, i) for i in devices if i - distance in devices]
    return lax.ppermute(block, axis, route)


MESH = pl.DeviceIdType.MESH
ORDER = (0, 17, 18, 19, 20, 1, 2, 3, 4, 5, 6, 7, 8, 9, 10, 11, 12, 13, 14, 15, 16, 21, 22, 23)
PLACE = {field: place for place, field in enumerate(ORDER)}
MIXED = 5
PORTIONS = 6
FACES = tuple(
    tuple(side if d == axis else 0 for d in range(3)) for axis in range(3) for side in (-1, 1)
)
EDGES = tuple(
    (dx, dy, dz)
    for dx in (-1, 0, 1)
    for dy in (-1, 0, 1)
    for dz in (-1, 0, 1)
    if abs(dx) + abs(dy) + abs(dz) == 2
)
ROUTES = FACES + EDGES


def slope(m2, m1, p1, p2):
    return (8.0 * (p1 - m1) - (p2 - m2)) * (1.0 / 12.0)


def step_kernel(
    shifts_ref, source_ref, moved_ref, filled_ref, out_ref, start_ref, gathered, column, box, zhalo, acc, slopes, ysend, yrecv, csend, crecv, zsend, zcore, zx, zy,
    send_sem, recv_sem, own_send, own_recv, far_send, far_recv, on_send, on_recv, y_send, y_recv,
):
    fields = start_ref.shape[0]
    portion = fields // PORTIONS
    groups = zsend.shape[2]
    counts = tuple(lax.axis_size(name) for name in ("gx", "gy", "gz"))
    place = tuple(lax.axis_index(name) for name in ("gx", "gy", "gz"))
    lane = lax.broadcasted_iota(jnp.int32, (8, 128), 1)
    row = lax.broadcasted_iota(jnp.int32, (8, 128), 0)
    zero = jnp.zeros((8, 128), jnp.float32)

    def present(route):
        ok = None
        for d in range(3):
            if route[d] != 0:
                here = place[d] > 0 if route[d] < 0 else place[d] < counts[d] - 1
                ok = here if ok is None else jnp.logical_and(ok, here)
        return ok

    def peer(route):
        return tuple(place[d] + route[d] for d in range(3))

    def opposite(route):
        return tuple(-side for side in route)

    def wipe_field(f, carry):
        for slot in range(2):
            for x in range(14):
                for y in (0, 16) if 3 <= x < 11 else (0, 8, 16):
                    box[slot, f, x, pl.ds(y, 8), :] = zero
        return carry

    lax.fori_loop(0, fields, wipe_field, 0)

    @pl.when(place[1] == counts[1] - 1)
    def _():
        def wipe_column(f, carry):
            for x in range(8):
                column[f, x, pl.ds(8, 8), :] = zero
            return carry

        lax.fori_loop(0, fields, wipe_column, 0)

    def keep_own(f, carry):
        for x in range(8):
            gathered[0, f, x] = filled_ref[f, x]
            column[f, x, pl.ds(0, 8), :] = moved_ref[f, x]
        return carry

    for slot in range(2):
        for z in range(2):
            for g in range(groups):
                zcore[slot, z, g] = zero
            for side in range(2):
                for g in range(2):
                    zx[slot, side, z, g] = zero
                    zy[slot, side, z, g] = zero
            for side in range(2):
                for f in range(MIXED):
                    crecv[slot, z, side, f] = zero

    def wipe_y(f, carry):
        for slot in range(2):
            for side in range(2):
                for j in range(3):
                    yrecv[slot, side, j, f] = zero
        return carry

    lax.fori_loop(0, fields, wipe_y, 0)

    barrier = pltpu.get_barrier_semaphore()
    partner = (place[0] + 1 - 2 * lax.rem(place[0], 2), place[1], place[2])
    across = (lax.rem(place[0] + 2, 4), place[1], place[2])
    total = jnp.int32(2)
    for other in (partner, across):
        pl.semaphore_signal(barrier, inc=1, device_id=other, device_id_type=MESH)
    for route in ROUTES:
        ok = present(route)
        total = total + ok.astype(jnp.int32)

        @pl.when(ok)
        def _(route=route):
            pl.semaphore_signal(barrier, inc=1, device_id=peer(route), device_id_type=MESH)

    pl.semaphore_wait(barrier, total)

    def remote(source, target, sent, got, device):
        return pltpu.make_async_remote_copy(
            src_ref=source,
            dst_ref=target,
            send_sem=sent,
            recv_sem=got,
            device_id=device,
            device_id_type=MESH,
        )

    def far_copy(k):
        part = pl.ds(k * portion, portion)
        return remote(
            filled_ref.at[part], gathered.at[2, part], far_send.at[k], far_recv.at[k], across
        )

    def on_copy(k):
        part = pl.ds(k * portion, portion)
        return remote(
            gathered.at[2, part], gathered.at[3, part], on_send.at[k], on_recv.at[k], partner
        )

    own_copy = remote(filled_ref, gathered.at[1], own_send, own_recv, partner)
    y_copy = remote(
        moved_ref,
        column.at[:, :, pl.ds(8, 8), :],
        y_send,
        y_recv,
        (place[0], place[1] - 1, place[2]),
    )

    @pl.when(place[1] > 0)
    def _():
        y_copy.start()

    for k in range(PORTIONS):
        far_copy(k).start()
    own_copy.start()
    lax.fori_loop(0, fields, keep_own, 0)
    for k in range(PORTIONS):
        far_copy(k).wait_recv()
        on_copy(k).start()
    own_copy.wait()
    for k in range(PORTIONS):
        on_copy(k).wait()
        far_copy(k).wait_send()

    @pl.when(place[1] > 0)
    def _():
        y_copy.wait_send()

    @pl.when(place[1] < counts[1] - 1)
    def _():
        y_copy.wait_recv()

    chosen = source_ref[0]
    shift_y = shifts_ref[1]
    row_spot = row + (place[1] * 8 + shifts_ref[1])
    column_entering = row_spot >= 8 * counts[1]
    for f in range(fields):
        for x in range(8):
            x_spot = jnp.zeros((8, 128), jnp.int32) + (place[0] * 8 + x + shifts_ref[0])
            entering = jnp.logical_or(column_entering, x_spot >= 8 * counts[0])
            name = ORDER[f]
            value = jnp.where(entering, gathered[chosen, name, x], column[name, x, pl.ds(shift_y, 8), :])
            start_ref[name, x] = value
            acc[name, x] = value
            box[0, f, 3 + x, pl.ds(8, 8), :] = value

    def message(number, slot):
        route = ROUTES[number]
        dx, dy, dz = route
        low = lambda side: 1 if side < 0 else 0
        high = lambda side: 0 if side < 0 else 1
        if dx != 0 and dy == 0 and dz == 0:
            source = box.at[slot, :, pl.ds(3 if dx < 0 else 8, 3), pl.ds(8, 8), :]
            target = box.at[slot, :, pl.ds(11 if dx < 0 else 0, 3), pl.ds(8, 8), :]
        elif dy != 0 and dx == 0 and dz == 0:
            source = ysend.at[slot, high(dy)]
            target = yrecv.at[slot, low(dy)]
        elif dz != 0 and dx == 0 and dy == 0:
            source = zsend.at[slot, high(dz)]
            target = zcore.at[slot, low(dz)]
        elif dz == 0:
            source = csend.at[slot, high(dy)]
            target = crecv.at[slot, low(dy), low(dx)]
        elif dy == 0:
            source = zsend.at[slot, high(dz), pl.ds(0, 2)]
            target = zx.at[slot, low(dx), low(dz)]
        else:
            source = zsend.at[slot, high(dz), pl.ds(0, 2)]
            target = zy.at[slot, low(dy), low(dz)]
        return pltpu.make_async_remote_copy(
            src_ref=source,
            dst_ref=target,
            send_sem=send_sem.at[number],
            recv_sem=recv_sem.at[slot, number],
            device_id=peer(route),
            device_id_type=MESH,
        )

    def launch(slot, wanted):
        for number, route in enumerate(ROUTES):
            if wanted(route):

                @pl.when(present(route))
                def _(number=number):
                    message(number, slot).start()

    def unpacked(from_low, from_high, t):
        return jnp.where(
            lane < 64,
            pltpu.roll(from_high, (128 - 4 * t) % 128, axis=1),
            pltpu.roll(from_low, (124 - 4 * t) % 128, axis=1),
        )

    def stage(s, carry):
        slot = lax.rem(s, 2)
        launch(slot, lambda r: r[1] == 0 and r[2] == 0)

        def pack_y(f, c):
            for j in range(3):
                ysend[slot, 0, j, f] = box[slot, f, pl.ds(3, 8), 8 + j, :]
                ysend[slot, 1, j, f] = box[slot, f, pl.ds(3, 8), 13 + j, :]
            return c

        lax.fori_loop(0, fields, pack_y, 0)
        launch(slot, lambda r: r[0] == 0 and r[2] == 0)
        outer = jnp.logical_or(row < 2, row >= 6)
        for side in range(2):
            for f in range(MIXED):
                csend[slot, side, f] = jnp.where(
                    outer,
                    ysend[slot, side, side, f],
                    pltpu.roll(ysend[slot, side, side + 1, f], 4, axis=0),
                )
        launch(slot, lambda r: r[2] == 0 and r[0] != 0 and r[1] != 0)

        def pack_z(g, c):
            low = zero
            high = zero
            for q in range(4):
                for x in range(8):
                    t = q * 8 + x
                    value = box[slot, 4 * g + q, 3 + x, pl.ds(8, 8), :]
                    inside = jnp.logical_and(lane >= 4 * t, lane < 4 * t + 4)
                    low = jnp.where(inside, pltpu.roll(value, 4 * t, axis=1), low)
                    high = jnp.where(inside, pltpu.roll(value, (4 * t + 4) % 128, axis=1), high)
            zsend[slot, 0, g] = low
            zsend[slot, 1, g] = high
            return c

        lax.fori_loop(0, groups, pack_z, 0)
        launch(slot, lambda r: r[2] != 0)

        for number, route in enumerate(ROUTES):

            @pl.when(present(opposite(route)))
            def _(number=number):
                message(number, slot).wait_recv()

        def spread_y(f, c):
            for j in range(3):
                box[slot, f, pl.ds(3, 8), 5 + j, :] = yrecv[slot, 0, j, f]
                box[slot, f, pl.ds(3, 8), 16 + j, :] = yrecv[slot, 1, j, f]
            return c

        lax.fori_loop(0, fields, spread_y, 0)
        for f in range(MIXED):
            for side, first_row in ((0, 6), (1, 16)):
                for j in range(2):
                    box[slot, f, pl.ds(1, 2), first_row + j, :] = crecv[
                        slot, side, 0, f, pl.ds(6 if j == 0 else 2, 2), :
                    ]
                    box[slot, f, pl.ds(11, 2), first_row + j, :] = crecv[
                        slot, side, 1, f, pl.ds(0 if j == 0 else 4, 2), :
                    ]

        def spread_z(g, c):
            from_low = zcore[slot, 0, g]
            from_high = zcore[slot, 1, g]
            for q in range(4):
                for x in range(8):
                    zhalo[4 * g + q, 2 + x, pl.ds(8, 8), :] = unpacked(
                        from_low, from_high, q * 8 + x
                    )
            return c

        lax.fori_loop(0, groups, spread_z, 0)
        for f in range(MIXED):
            g, q = f // 4, f % 4
            for side in range(2):
                low_x, high_x = zx[slot, side, 0, g], zx[slot, side, 1, g]
                for k in range(2):
                    x = 6 + k if side == 0 else k
                    at = k if side == 0 else 10 + k
                    zhalo[f, at, pl.ds(8, 8), :] = unpacked(low_x, high_x, q * 8 + x)
                low_y, high_y = zy[slot, side, 0, g], zy[slot, side, 1, g]
                for x in range(8):
                    zhalo[f, 2 + x, pl.ds(16 * side, 8), :] = unpacked(low_y, high_y, q * 8 + x)

        share = jnp.where(jnp.logical_or(s == 0, s == 3), STEP / 6.0, STEP / 3.0)
        share = share.astype(jnp.float32)
        reach = jnp.where(s == 2, STEP, 0.5 * STEP).astype(jnp.float32)
        later = 1 - slot

        def slab(x, c):
            def at_z(value, halo, amount):
                if amount > 0:
                    return pltpu.roll(jnp.where(lane < amount, halo, value), 128 - amount, axis=1)
                return pltpu.roll(
                    jnp.where(lane >= 128 + amount, halo, value), -amount, axis=1
                )

            def tile(f, dx=0, dy=0):
                return box[slot, f, 3 + x + dx, pl.ds(8 + dy, 8), :]

            def slope_z(value, halo):
                return slope(*(at_z(value, halo, amount) for amount in (-2, -1, 1, 2)))

            def study(name, gradient=False):
                f = PLACE[name]
                centre = tile(f)
                halo = zhalo[f, 2 + x, pl.ds(8, 8), :]
                pairs = []
                grads = []
                for d in range(3):
                    cells = {}
                    for amount in (-3, -2, -1, 1, 2, 3):
                        if d == 0:
                            cells[amount] = tile(f, amount, 0)
                        elif d == 1:
                            cells[amount] = tile(f, 0, amount)
                        else:
                            cells[amount] = at_z(centre, halo, amount)
                    pairs.append([cells[k] + cells[-k] for k in (1, 2, 3)])
                    if gradient:
                        grads.append(slope(cells[-2], cells[-1], cells[1], cells[2]))
                ones, twos, threes = [pairs[0][k] + pairs[1][k] + pairs[2][k] for k in range(3)]
                damp = (threes - 6.0 * twos + 15.0 * ones - 60.0 * centre) * (SIGMA / 64.0)
                lap = (16.0 * ones - twos - 90.0 * centre) * (1.0 / 12.0)
                curves = [
                    (16.0 * pairs[d][0] - pairs[d][1] - 30.0 * centre) * (1.0 / 12.0)
                    for d in range(3)
                ]
                return centre, damp, lap, curves, grads

            def finish(name, rate):
                f = PLACE[name]
                total = acc[name, x] + share * rate
                acc[name, x] = total
                box[later, f, 3 + x, pl.ds(8, 8), :] = start_ref[name, x] + reach * rate

            def across_x(name, y):
                f = PLACE[name]
                return slope(
                    *(box[slot, f, 3 + x + k, pl.ds(y, 8), :] for k in (-2, -1, 1, 2))
                )

            def halo_x(name):
                f = PLACE[name]
                return slope(
                    *(zhalo[f, 2 + x + k, pl.ds(8, 8), :] for k in (-2, -1, 1, 2))
                )

            def along_y(name):
                f = PLACE[name]
                return slope(*(tile(f, 0, k) for k in (-2, -1, 1, 2)))

            def halo_y(name):
                f = PLACE[name]
                return slope(
                    *(zhalo[f, 2 + x, pl.ds(8 + k, 8), :] for k in (-2, -1, 1, 2))
                )

            def mixed_xy(number, value):
                for y in (0, 8, 16):
                    slopes[number, pl.ds(y, 8), :] = value(lambda name: across_x(name, y))
                return slope(*(slopes[number, pl.ds(8 + k, 8), :] for k in (-2, -1, 1, 2)))

            def mixed_xz(value):
                return slope_z(value(lambda name: across_x(name, 8)), value(halo_x))

            def mixed_yz(value):
                return slope_z(value(along_y), value(halo_y))

            both = lambda part: part(17) + 2.0 * part(0)
            only = lambda name: (lambda part: part(name))

            curv, curv_damp, _, _, curv_grad = study(7, True)
            phi, phi_damp, _, phi_curves, _ = study(0)
            lapse, lapse_damp, lapse_lap, lapse_curves, _ = study(17)
            finish(17, lapse_damp - 2.0 * curv)
            finish(7, curv_damp - lapse_lap)
            shift_parts = [study(18 + i, True) for i in range(3)]
            shift_grad = [[shift_parts[j][4][d] for j in range(3)] for d in range(3)]
            spread = shift_grad[0][0] + shift_grad[1][1] + shift_grad[2][2]
            finish(0, phi_damp + (spread - curv) * (1.0 / 6.0))
            crossed = (
                mixed_xy(0, only(19)) + mixed_xz(only(20)),
                mixed_xy(1, only(18)) + mixed_yz(only(20)),
                mixed_xz(only(18)) + mixed_yz(only(19)),
            )
            gamma_grad = []
            gamma_parts = [study(14 + i, True) for i in range(3)]
            gamma_grad = [[gamma_parts[j][4][d] for j in range(3)] for d in range(3)]
            for i in range(3):
                rate = (
                    shift_parts[i][2]
                    - (4.0 / 3.0) * curv_grad[i]
                    + (shift_parts[i][3][i] + crossed[i]) * (1.0 / 3.0)
                )
                finish(14 + i, rate + gamma_parts[i][1])
                driver, driver_damp, _, _, _ = study(21 + i)
                finish(18 + i, shift_parts[i][1] + 0.75 * driver)
                finish(21 + i, driver_damp + rate - DRIVER_DAMP * driver)
            hessian = {
                (0, 1): mixed_xy(2, both),
                (0, 2): mixed_xz(both),
                (1, 2): mixed_yz(both),
            }
            for i in range(3):
                hessian[(i, i)] = lapse_curves[i] + 2.0 * phi_curves[i]
            ricci = []
            free_damp = []
            for n, (i, j) in enumerate(PAIRS):
                free, damp, _, _, _ = study(8 + n)
                free_damp.append(damp)
                _, metric_damp, metric_lap, _, _ = study(1 + n)
                value = shift_grad[i][j] + shift_grad[j][i] - 2.0 * free
                if i == j:
                    value = value - (2.0 / 3.0) * spread
                finish(1 + n, value + metric_damp)
                ricci.append(
                    0.5 * (gamma_grad[i][j] + gamma_grad[j][i] - metric_lap) - hessian[(i, j)]
                )
            trace = (ricci[0] + ricci[3] + ricci[5]) * (1.0 / 3.0)
            for n, (i, j) in enumerate(PAIRS):
                value = ricci[n] - trace if i == j else ricci[n]
                finish(8 + n, value + free_damp[n])
            return c

        lax.fori_loop(0, 8, slab, 0)
        for number, route in enumerate(ROUTES):

            @pl.when(present(route))
            def _(number=number):
                message(number, slot).wait_send()

        return carry

    lax.fori_loop(0, 4, stage, 0)

    def hand_out(f, carry):
        for x in range(8):
            out_ref[f, x] = acc[f, x]
        return carry

    lax.fori_loop(0, fields, hand_out, 0)


def advance(shifts, source, moved, filled):
    fields, width, height, depth = moved.shape
    groups = fields * width // 32
    tall = height + 16

    def buffer(*sizes):
        return pltpu.VMEM(sizes + (depth,), jnp.float32)

    return pl.pallas_call(
        step_kernel,
        out_shape=jax.ShapeDtypeStruct(moved.shape, jnp.float32),
        in_specs=[pl.BlockSpec(memory_space=pltpu.SMEM)] * 2
        + [pl.BlockSpec(memory_space=pltpu.VMEM)] * 2,
        out_specs=pl.BlockSpec(memory_space=pltpu.VMEM),
        scratch_shapes=[
            buffer(fields, width, height),
            buffer(4, fields, width, height),
            buffer(fields, width, 2 * height),
            buffer(2, fields, width + 6, tall),
            buffer(fields, width + 4, tall),
            buffer(fields, width, height),
            buffer(3, tall),
            buffer(2, 2, 3, fields, width),
            buffer(2, 2, 3, fields, width),
            buffer(2, 2, MIXED, width),
            buffer(2, 2, 2, MIXED, width),
            buffer(2, 2, groups, height),
            buffer(2, 2, groups, height),
            buffer(2, 2, 2, 2, height),
            buffer(2, 2, 2, 2, height),
            pltpu.SemaphoreType.DMA((len(ROUTES),)),
            pltpu.SemaphoreType.DMA((2, len(ROUTES))),
            pltpu.SemaphoreType.DMA,
            pltpu.SemaphoreType.DMA,
            pltpu.SemaphoreType.DMA((PORTIONS,)),
            pltpu.SemaphoreType.DMA((PORTIONS,)),
            pltpu.SemaphoreType.DMA((PORTIONS,)),
            pltpu.SemaphoreType.DMA((PORTIONS,)),
            pltpu.SemaphoreType.DMA,
            pltpu.SemaphoreType.DMA,
        ],
        compiler_params=pltpu.CompilerParams(
            collective_id=0, has_side_effects=True, vmem_limit_bytes=48 * 1024 * 1024
        ),
    )(shifts, source, moved, filled)


def lagrange(shift, rows, cols):
    matrix = np.zeros((rows, cols), np.float32)
    for line in range(rows):
        spot = line + shift
        first = spot // 2 + spot % 2
        for t, weight in enumerate(ODD_W if spot % 2 else EVEN_W):
            if first + t < cols:
                matrix[line, first + t] = weight
    return matrix


def lagrange_at(shift, rows, cols):
    table = np.stack([lagrange(s, rows, cols) for s in range(rows + 1)])
    return lax.dynamic_index_in_dim(jnp.asarray(table), shift, 0, keepdims=False)


def flatten_kernel(bricks_ref, flat_ref, sem):
    copy = pltpu.make_async_copy(bricks_ref.at[0, 0, 0], flat_ref, sem)
    copy.start()
    copy.wait()


def flattened(bricks):
    return pl.pallas_call(
        flatten_kernel,
        out_shape=jax.ShapeDtypeStruct((bricks.size,), jnp.float32),
        in_specs=[pl.BlockSpec(memory_space=pl.ANY)],
        out_specs=pl.BlockSpec(memory_space=pl.ANY),
        scratch_shapes=[pltpu.SemaphoreType.DMA],
    )(bricks)


def body(state, coarse_bricks, shifts, brick_owner):
    fields, width, height, depth = state.shape
    brick_side = width + 4
    brick_depth = depth // 2 + 4
    shift_x = shifts[0]
    shift_y = shifts[1]
    beyond_x = passed_along(state, "gx", -1)
    moved = lax.dynamic_slice_in_dim(
        jnp.concatenate([state, beyond_x], axis=1), shift_x, width, axis=1
    )
    place_x = lax.axis_index("gx")
    wanted = jnp.sum(
        jnp.where(jnp.arange(brick_owner.shape[0], dtype=jnp.int32) == place_x, brick_owner, 0)
    )
    brick = flattened(coarse_bricks).reshape((fields, brick_side, brick_side, brick_depth))
    along_x = lagrange_at(shift_x, width, brick_side)
    along_y = lagrange_at(shift_y, height, brick_side)
    along_z = jnp.asarray(lagrange(0, depth, brick_depth))
    first_pass = jnp.einsum("fpqr,kr->fpqk", brick, along_z, precision=HIGH)
    second_pass = jnp.einsum("fpqk,jq->fpjk", first_pass, along_y, precision=HIGH)
    filled = jnp.einsum("fpjk,ip->fijk", second_pass, along_x, precision=HIGH)
    source = jnp.bitwise_xor(wanted, place_x).astype(jnp.int32).reshape(1)
    return advance(shifts, source, moved, filled)


def solution(mesh):
    return jax.shard_map(
        body,
        mesh=mesh,
        in_specs=(P(None, "gx", "gy", "gz"), P("gx", "gy", "gz", None), P(), P()),
        out_specs=P(None, "gx", "gy", "gz"),
        check_vma=False,
    )
```

```python
import jax
import jax.numpy as jnp
import numpy as np
from jax import lax
from jax.experimental import pallas as pl
from jax.experimental.pallas import tpu as pltpu
from jax.sharding import PartitionSpec as P

EVEN_W = (-0.0390625, 0.2734375, 0.8203125, -0.0546875)
ODD_W = (-0.0546875, 0.8203125, 0.2734375, -0.0390625)
PAIRS = ((0, 0), (0, 1), (0, 2), (1, 1), (1, 2), (2, 2))
SIGMA = 0.3
DRIVER_DAMP = 2.0
STEP = 0.25
HIGH = lax.Precision.HIGHEST


def passed_along(block, axis, distance):
    devices = range(lax.axis_size(axis))
    route = [(i - distance, i) for i in devices if i - distance in devices]
    return lax.ppermute(block, axis, route)


MESH = pl.DeviceIdType.MESH
ORDER = (0, 17, 18, 19, 20, 1, 2, 3, 4, 5, 6, 7, 8, 9, 10, 11, 12, 13, 14, 15, 16, 21, 22, 23)
PLACE = {field: place for place, field in enumerate(ORDER)}
MIXED = 5
PORTIONS = 6
FACES = tuple(
    tuple(side if d == axis else 0 for d in range(3)) for axis in range(3) for side in (-1, 1)
)
EDGES = tuple(
    (dx, dy, dz)
    for dx in (-1, 0, 1)
    for dy in (-1, 0, 1)
    for dz in (-1, 0, 1)
    if abs(dx) + abs(dy) + abs(dz) == 2
)
ROUTES = FACES + EDGES


def slope(m2, m1, p1, p2):
    return (8.0 * (p1 - m1) - (p2 - m2)) * (1.0 / 12.0)


def step_kernel(
    shifts_ref, source_ref, moved_ref, filled_ref, out_ref, start_ref, gathered, column, box, zhalo, acc, slopes, ysend, yrecv, csend, crecv, zsend, zcore, zx, zy,
    send_sem, recv_sem, own_send, own_recv, far_send, far_recv, on_send, on_recv, y_send, y_recv,
):
    fields = start_ref.shape[0]
    portion = fields // PORTIONS
    groups = zsend.shape[2]
    counts = tuple(lax.axis_size(name) for name in ("gx", "gy", "gz"))
    place = tuple(lax.axis_index(name) for name in ("gx", "gy", "gz"))
    lane = lax.broadcasted_iota(jnp.int32, (8, 128), 1)
    row = lax.broadcasted_iota(jnp.int32, (8, 128), 0)
    zero = jnp.zeros((8, 128), jnp.float32)

    def present(route):
        ok = None
        for d in range(3):
            if route[d] != 0:
                here = place[d] > 0 if route[d] < 0 else place[d] < counts[d] - 1
                ok = here if ok is None else jnp.logical_and(ok, here)
        return ok

    def peer(route):
        return tuple(place[d] + route[d] for d in range(3))

    def opposite(route):
        return tuple(-side for side in route)

    def wipe_field(f, carry):
        for slot in range(2):
            for x in range(14):
                for y in (0, 16) if 3 <= x < 11 else (0, 8, 16):
                    box[slot, f, x, pl.ds(y, 8), :] = zero
        return carry

    lax.fori_loop(0, fields, wipe_field, 0)

    @pl.when(place[1] == counts[1] - 1)
    def _():
        def wipe_column(f, carry):
            for x in range(8):
                column[f, x, pl.ds(8, 8), :] = zero
            return carry

        lax.fori_loop(0, fields, wipe_column, 0)

    def keep_own(f, carry):
        for x in range(8):
            gathered[0, f, x] = filled_ref[f, x]
            column[f, x, pl.ds(0, 8), :] = moved_ref[f, x]
        return carry

    for slot in range(2):
        for z in range(2):
            for g in range(groups):
                zcore[slot, z, g] = zero
            for side in range(2):
                for g in range(2):
                    zx[slot, side, z, g] = zero
                    zy[slot, side, z, g] = zero
            for side in range(2):
                for f in range(MIXED):
                    crecv[slot, z, side, f] = zero

    def wipe_y(f, carry):
        for slot in range(2):
            for side in range(2):
                for j in range(3):
                    yrecv[slot, side, j, f] = zero
        return carry

    lax.fori_loop(0, fields, wipe_y, 0)

    barrier = pltpu.get_barrier_semaphore()
    partner = (place[0] + 1 - 2 * lax.rem(place[0], 2), place[1], place[2])
    across = (lax.rem(place[0] + 2, 4), place[1], place[2])
    total = jnp.int32(2)
    for other in (partner, across):
        pl.semaphore_signal(barrier, inc=1, device_id=other, device_id_type=MESH)
    for route in ROUTES:
        ok = present(route)
        total = total + ok.astype(jnp.int32)

        @pl.when(ok)
        def _(route=route):
            pl.semaphore_signal(barrier, inc=1, device_id=peer(route), device_id_type=MESH)

    pl.semaphore_wait(barrier, total)

    def remote(source, target, sent, got, device):
        return pltpu.make_async_remote_copy(
            src_ref=source,
            dst_ref=target,
            send_sem=sent,
            recv_sem=got,
            device_id=device,
            device_id_type=MESH,
        )

    def far_copy(k):
        part = pl.ds(k * portion, portion)
        return remote(
            filled_ref.at[part], gathered.at[2, part], far_send.at[k], far_recv.at[k], across
        )

    def on_copy(k):
        part = pl.ds(k * portion, portion)
        return remote(
            gathered.at[2, part], gathered.at[3, part], on_send.at[k], on_recv.at[k], partner
        )

    own_copy = remote(filled_ref, gathered.at[1], own_send, own_recv, partner)
    y_copy = remote(
        moved_ref,
        column.at[:, :, pl.ds(8, 8), :],
        y_send,
        y_recv,
        (place[0], place[1] - 1, place[2]),
    )

    @pl.when(place[1] > 0)
    def _():
        y_copy.start()

    for k in range(PORTIONS):
        far_copy(k).start()
    own_copy.start()
    lax.fori_loop(0, fields, keep_own, 0)
    for k in range(PORTIONS):
        far_copy(k).wait_recv()
        on_copy(k).start()
    own_copy.wait()
    for k in range(PORTIONS):
        on_copy(k).wait()
        far_copy(k).wait_send()

    @pl.when(place[1] > 0)
    def _():
        y_copy.wait_send()

    @pl.when(place[1] < counts[1] - 1)
    def _():
        y_copy.wait_recv()

    chosen = source_ref[0]
    shift_y = shifts_ref[1]
    row_spot = row + (place[1] * 8 + shifts_ref[1])
    column_entering = row_spot >= 8 * counts[1]
    for f in range(fields):
        for x in range(8):
            x_spot = jnp.zeros((8, 128), jnp.int32) + (place[0] * 8 + x + shifts_ref[0])
            entering = jnp.logical_or(column_entering, x_spot >= 8 * counts[0])
            name = ORDER[f]
            value = jnp.where(entering, gathered[chosen, name, x], column[name, x, pl.ds(shift_y, 8), :])
            start_ref[name, x] = value
            acc[name, x] = value
            box[0, f, 3 + x, pl.ds(8, 8), :] = value

    def message(number, slot):
        route = ROUTES[number]
        dx, dy, dz = route
        low = lambda side: 1 if side < 0 else 0
        high = lambda side: 0 if side < 0 else 1
        if dx != 0 and dy == 0 and dz == 0:
            source = box.at[slot, :, pl.ds(3 if dx < 0 else 8, 3), pl.ds(8, 8), :]
            target = box.at[slot, :, pl.ds(11 if dx < 0 else 0, 3), pl.ds(8, 8), :]
        elif dy != 0 and dx == 0 and dz == 0:
            source = ysend.at[slot, high(dy)]
            target = yrecv.at[slot, low(dy)]
        elif dz != 0 and dx == 0 and dy == 0:
            source = zsend.at[slot, high(dz)]
            target = zcore.at[slot, low(dz)]
        elif dz == 0:
            source = csend.at[slot, high(dy)]
            target = crecv.at[slot, low(dy), low(dx)]
        elif dy == 0:
            source = zsend.at[slot, high(dz), pl.ds(0, 2)]
            target = zx.at[slot, low(dx), low(dz)]
        else:
            source = zsend.at[slot, high(dz), pl.ds(0, 2)]
            target = zy.at[slot, low(dy), low(dz)]
        return pltpu.make_async_remote_copy(
            src_ref=source,
            dst_ref=target,
            send_sem=send_sem.at[number],
            recv_sem=recv_sem.at[slot, number],
            device_id=peer(route),
            device_id_type=MESH,
        )

    def launch(slot, wanted):
        for number, route in enumerate(ROUTES):
            if wanted(route):

                @pl.when(present(route))
                def _(number=number):
                    message(number, slot).start()

    def unpacked(from_low, from_high, t):
        return jnp.where(
            lane < 64,
            pltpu.roll(from_high, (128 - 4 * t) % 128, axis=1),
            pltpu.roll(from_low, (124 - 4 * t) % 128, axis=1),
        )

    def stage(s, carry):
        slot = lax.rem(s, 2)
        launch(slot, lambda r: r[1] == 0 and r[2] == 0)

        def pack_y(f, c):
            for j in range(3):
                ysend[slot, 0, j, f] = box[slot, f, pl.ds(3, 8), 8 + j, :]
                ysend[slot, 1, j, f] = box[slot, f, pl.ds(3, 8), 13 + j, :]
            return c

        lax.fori_loop(0, fields, pack_y, 0)
        launch(slot, lambda r: r[0] == 0 and r[2] == 0)
        outer = jnp.logical_or(row < 2, row >= 6)
        for side in range(2):
            for f in range(MIXED):
                csend[slot, side, f] = jnp.where(
                    outer,
                    ysend[slot, side, side, f],
                    pltpu.roll(ysend[slot, side, side + 1, f], 4, axis=0),
                )
        launch(slot, lambda r: r[2] == 0 and r[0] != 0 and r[1] != 0)

        def pack_z(g, c):
            low = zero
            high = zero
            for q in range(4):
                for x in range(8):
                    t = q * 8 + x
                    value = box[slot, 4 * g + q, 3 + x, pl.ds(8, 8), :]
                    inside = jnp.logical_and(lane >= 4 * t, lane < 4 * t + 4)
                    low = jnp.where(inside, pltpu.roll(value, 4 * t, axis=1), low)
                    high = jnp.where(inside, pltpu.roll(value, (4 * t + 4) % 128, axis=1), high)
            zsend[slot, 0, g] = low
            zsend[slot, 1, g] = high
            return c

        lax.fori_loop(0, groups, pack_z, 0)
        launch(slot, lambda r: r[2] != 0)

        for number, route in enumerate(ROUTES):

            @pl.when(present(opposite(route)))
            def _(number=number):
                message(number, slot).wait_recv()

        def spread_y(f, c):
            for j in range(3):
                box[slot, f, pl.ds(3, 8), 5 + j, :] = yrecv[slot, 0, j, f]
                box[slot, f, pl.ds(3, 8), 16 + j, :] = yrecv[slot, 1, j, f]
            return c

        lax.fori_loop(0, fields, spread_y, 0)
        for f in range(MIXED):
            for side, first_row in ((0, 6), (1, 16)):
                for j in range(2):
                    box[slot, f, pl.ds(1, 2), first_row + j, :] = crecv[
                        slot, side, 0, f, pl.ds(6 if j == 0 else 2, 2), :
                    ]
                    box[slot, f, pl.ds(11, 2), first_row + j, :] = crecv[
                        slot, side, 1, f, pl.ds(0 if j == 0 else 4, 2), :
                    ]

        def spread_z(g, c):
            from_low = zcore[slot, 0, g]
            from_high = zcore[slot, 1, g]
            for q in range(4):
                for x in range(8):
                    zhalo[4 * g + q, 2 + x, pl.ds(8, 8), :] = unpacked(
                        from_low, from_high, q * 8 + x
                    )
            return c

        lax.fori_loop(0, groups, spread_z, 0)
        for f in range(MIXED):
            g, q = f // 4, f % 4
            for side in range(2):
                low_x, high_x = zx[slot, side, 0, g], zx[slot, side, 1, g]
                for k in range(2):
                    x = 6 + k if side == 0 else k
                    at = k if side == 0 else 10 + k
                    zhalo[f, at, pl.ds(8, 8), :] = unpacked(low_x, high_x, q * 8 + x)
                low_y, high_y = zy[slot, side, 0, g], zy[slot, side, 1, g]
                for x in range(8):
                    zhalo[f, 2 + x, pl.ds(16 * side, 8), :] = unpacked(low_y, high_y, q * 8 + x)

        share = jnp.where(jnp.logical_or(s == 0, s == 3), STEP / 6.0, STEP / 3.0)
        share = share.astype(jnp.float32)
        reach = jnp.where(s == 2, STEP, 0.5 * STEP).astype(jnp.float32)
        later = 1 - slot

        def slab(x, c):
            def at_z(value, halo, amount):
                if amount > 0:
                    return pltpu.roll(jnp.where(lane < amount, halo, value), 128 - amount, axis=1)
                return pltpu.roll(
                    jnp.where(lane >= 128 + amount, halo, value), -amount, axis=1
                )

            def tile(f, dx=0, dy=0):
                return box[slot, f, 3 + x + dx, pl.ds(8 + dy, 8), :]

            def slope_z(value, halo):
                return slope(*(at_z(value, halo, amount) for amount in (-2, -1, 1, 2)))

            def study(name, gradient=False):
                f = PLACE[name]
                centre = tile(f)
                halo = zhalo[f, 2 + x, pl.ds(8, 8), :]
                pairs = []
                grads = []
                for d in range(3):
                    cells = {}
                    for amount in (-3, -2, -1, 1, 2, 3):
                        if d == 0:
                            cells[amount] = tile(f, amount, 0)
                        elif d == 1:
                            cells[amount] = tile(f, 0, amount)
                        else:
                            cells[amount] = at_z(centre, halo, amount)
                    pairs.append([cells[k] + cells[-k] for k in (1, 2, 3)])
                    if gradient:
                        grads.append(slope(cells[-2], cells[-1], cells[1], cells[2]))
                ones, twos, threes = [pairs[0][k] + pairs[1][k] + pairs[2][k] for k in range(3)]
                damp = (threes - 6.0 * twos + 15.0 * ones - 60.0 * centre) * (SIGMA / 64.0)
                lap = (16.0 * ones - twos - 90.0 * centre) * (1.0 / 12.0)
                curves = [
                    (16.0 * pairs[d][0] - pairs[d][1] - 30.0 * centre) * (1.0 / 12.0)
                    for d in range(3)
                ]
                return centre, damp, lap, curves, grads

            def finish(name, rate):
                f = PLACE[name]
                total = acc[name, x] + share * rate
                acc[name, x] = total
                box[later, f, 3 + x, pl.ds(8, 8), :] = start_ref[name, x] + reach * rate

            def across_x(name, y):
                f = PLACE[name]
                return slope(
                    *(box[slot, f, 3 + x + k, pl.ds(y, 8), :] for k in (-2, -1, 1, 2))
                )

            def halo_x(name):
                f = PLACE[name]
                return slope(
                    *(zhalo[f, 2 + x + k, pl.ds(8, 8), :] for k in (-2, -1, 1, 2))
                )

            def along_y(name):
                f = PLACE[name]
                return slope(*(tile(f, 0, k) for k in (-2, -1, 1, 2)))

            def halo_y(name):
                f = PLACE[name]
                return slope(
                    *(zhalo[f, 2 + x, pl.ds(8 + k, 8), :] for k in (-2, -1, 1, 2))
                )

            def mixed_xy(number, value):
                for y in (0, 8, 16):
                    slopes[number, pl.ds(y, 8), :] = value(lambda name: across_x(name, y))
                return slope(*(slopes[number, pl.ds(8 + k, 8), :] for k in (-2, -1, 1, 2)))

            def mixed_xz(value):
                return slope_z(value(lambda name: across_x(name, 8)), value(halo_x))

            def mixed_yz(value):
                return slope_z(value(along_y), value(halo_y))

            both = lambda part: part(17) + 2.0 * part(0)
            only = lambda name: (lambda part: part(name))

            curv, curv_damp, _, _, curv_grad = study(7, True)
            phi, phi_damp, _, phi_curves, _ = study(0)
            lapse, lapse_damp, lapse_lap, lapse_curves, _ = study(17)
            finish(17, lapse_damp - 2.0 * curv)
            finish(7, curv_damp - lapse_lap)
            shift_parts = [study(18 + i, True) for i in range(3)]
            shift_grad = [[shift_parts[j][4][d] for j in range(3)] for d in range(3)]
            spread = shift_grad[0][0] + shift_grad[1][1] + shift_grad[2][2]
            finish(0, phi_damp + (spread - curv) * (1.0 / 6.0))
            crossed = (
                mixed_xy(0, only(19)) + mixed_xz(only(20)),
                mixed_xy(1, only(18)) + mixed_yz(only(20)),
                mixed_xz(only(18)) + mixed_yz(only(19)),
            )
            gamma_grad = []
            gamma_parts = [study(14 + i, True) for i in range(3)]
            gamma_grad = [[gamma_parts[j][4][d] for j in range(3)] for d in range(3)]
            for i in range(3):
                rate = (
                    shift_parts[i][2]
                    - (4.0 / 3.0) * curv_grad[i]
                    + (shift_parts[i][3][i] + crossed[i]) * (1.0 / 3.0)
                )
                finish(14 + i, rate + gamma_parts[i][1])
                driver, driver_damp, _, _, _ = study(21 + i)
                finish(18 + i, shift_parts[i][1] + 0.75 * driver)
                finish(21 + i, driver_damp + rate - DRIVER_DAMP * driver)
            hessian = {
                (0, 1): mixed_xy(2, both),
                (0, 2): mixed_xz(both),
                (1, 2): mixed_yz(both),
            }
            for i in range(3):
                hessian[(i, i)] = lapse_curves[i] + 2.0 * phi_curves[i]
            ricci = []
            free_damp = []
            for n, (i, j) in enumerate(PAIRS):
                free, damp, _, _, _ = study(8 + n)
                free_damp.append(damp)
                _, metric_damp, metric_lap, _, _ = study(1 + n)
                value = shift_grad[i][j] + shift_grad[j][i] - 2.0 * free
                if i == j:
                    value = value - (2.0 / 3.0) * spread
                finish(1 + n, value + metric_damp)
                ricci.append(
                    0.5 * (gamma_grad[i][j] + gamma_grad[j][i] - metric_lap) - hessian[(i, j)]
                )
            trace = (ricci[0] + ricci[3] + ricci[5]) * (1.0 / 3.0)
            for n, (i, j) in enumerate(PAIRS):
                value = ricci[n] - trace if i == j else ricci[n]
                finish(8 + n, value + free_damp[n])
            return c

        lax.fori_loop(0, 8, slab, 0)
        for number, route in enumerate(ROUTES):

            @pl.when(present(route))
            def _(number=number):
                message(number, slot).wait_send()

        return carry

    lax.fori_loop(0, 4, stage, 0)

    def hand_out(f, carry):
        for x in range(8):
            out_ref[f, x] = acc[f, x]
        return carry

    lax.fori_loop(0, fields, hand_out, 0)


def advance(shifts, source, moved, filled):
    fields, width, height, depth = moved.shape
    groups = fields * width // 32
    tall = height + 16

    def buffer(*sizes):
        return pltpu.VMEM(sizes + (depth,), jnp.float32)

    return pl.pallas_call(
        step_kernel,
        out_shape=jax.ShapeDtypeStruct(moved.shape, jnp.float32),
        in_specs=[pl.BlockSpec(memory_space=pltpu.SMEM)] * 2
        + [pl.BlockSpec(memory_space=pltpu.VMEM)] * 2,
        out_specs=pl.BlockSpec(memory_space=pltpu.VMEM),
        scratch_shapes=[
            buffer(fields, width, height),
            buffer(4, fields, width, height),
            buffer(fields, width, 2 * height),
            buffer(2, fields, width + 6, tall),
            buffer(fields, width + 4, tall),
            buffer(fields, width, height),
            buffer(3, tall),
            buffer(2, 2, 3, fields, width),
            buffer(2, 2, 3, fields, width),
            buffer(2, 2, MIXED, width),
            buffer(2, 2, 2, MIXED, width),
            buffer(2, 2, groups, height),
            buffer(2, 2, groups, height),
            buffer(2, 2, 2, 2, height),
            buffer(2, 2, 2, 2, height),
            pltpu.SemaphoreType.DMA((len(ROUTES),)),
            pltpu.SemaphoreType.DMA((2, len(ROUTES))),
            pltpu.SemaphoreType.DMA,
            pltpu.SemaphoreType.DMA,
            pltpu.SemaphoreType.DMA((PORTIONS,)),
            pltpu.SemaphoreType.DMA((PORTIONS,)),
            pltpu.SemaphoreType.DMA((PORTIONS,)),
            pltpu.SemaphoreType.DMA((PORTIONS,)),
            pltpu.SemaphoreType.DMA,
            pltpu.SemaphoreType.DMA,
        ],
        compiler_params=pltpu.CompilerParams(
            collective_id=0, has_side_effects=True, vmem_limit_bytes=48 * 1024 * 1024
        ),
    )(shifts, source, moved, filled)


def lagrange(shift, rows, cols):
    matrix = np.zeros((rows, cols), np.float32)
    for line in range(rows):
        spot = line + shift
        first = spot // 2 + spot % 2
        for t, weight in enumerate(ODD_W if spot % 2 else EVEN_W):
            if first + t < cols:
                matrix[line, first + t] = weight
    return matrix


def lagrange_at(shift, rows, cols):
    table = np.stack([lagrange(s, rows, cols) for s in range(rows + 1)])
    return lax.dynamic_index_in_dim(jnp.asarray(table), shift, 0, keepdims=False)


def body(state, coarse_bricks, shifts, brick_owner):
    fields, width, height, depth = state.shape
    brick_side = width + 4
    brick_depth = depth // 2 + 4
    shift_x = shifts[0]
    shift_y = shifts[1]
    beyond_x = passed_along(state, "gx", -1)
    moved = lax.dynamic_slice_in_dim(
        jnp.concatenate([state, beyond_x], axis=1), shift_x, width, axis=1
    )
    place_x = lax.axis_index("gx")
    wanted = jnp.sum(
        jnp.where(jnp.arange(brick_owner.shape[0], dtype=jnp.int32) == place_x, brick_owner, 0)
    )
    brick = coarse_bricks.reshape((fields, brick_side, brick_side, brick_depth))
    along_x = lagrange_at(shift_x, width, brick_side)
    along_y = lagrange_at(shift_y, height, brick_side)
    along_z = jnp.asarray(lagrange(0, depth, brick_depth))
    first_pass = jnp.einsum("fpqr,kr->fpqk", brick, along_z, precision=HIGH)
    second_pass = jnp.einsum("fpqk,jq->fpjk", first_pass, along_y, precision=HIGH)
    filled = jnp.einsum("fpjk,ip->fijk", second_pass, along_x, precision=HIGH)
    source = jnp.bitwise_xor(wanted, place_x).astype(jnp.int32).reshape(1)
    return advance(shifts, source, moved, filled)


def solution(mesh):
    return jax.shard_map(
        body,
        mesh=mesh,
        in_specs=(P(None, "gx", "gy", "gz"), P("gx", "gy", "gz", None), P(), P()),
        out_specs=P(None, "gx", "gy", "gz"),
        check_vma=False,
    )
```

```python
import jax
import jax.numpy as jnp
import numpy as np
from jax import lax
from jax.experimental import pallas as pl
from jax.experimental.pallas import tpu as pltpu
from jax.sharding import PartitionSpec as P

EVEN_W = (-0.0390625, 0.2734375, 0.8203125, -0.0546875)
ODD_W = (-0.0546875, 0.8203125, 0.2734375, -0.0390625)
PAIRS = ((0, 0), (0, 1), (0, 2), (1, 1), (1, 2), (2, 2))
SIGMA = 0.3
DRIVER_DAMP = 2.0
STEP = 0.25
HIGH = lax.Precision.HIGHEST


def passed_along(block, axis, distance):
    devices = range(lax.axis_size(axis))
    route = [(i - distance, i) for i in devices if i - distance in devices]
    return lax.ppermute(block, axis, route)


MESH = pl.DeviceIdType.MESH
ORDER = (0, 17, 18, 19, 20, 1, 2, 3, 4, 5, 6, 7, 8, 9, 10, 11, 12, 13, 14, 15, 16, 21, 22, 23)
PLACE = {field: place for place, field in enumerate(ORDER)}
MIXED = 5
PORTIONS = 6
FACES = tuple(
    tuple(side if d == axis else 0 for d in range(3)) for axis in range(3) for side in (-1, 1)
)
EDGES = tuple(
    (dx, dy, dz)
    for dx in (-1, 0, 1)
    for dy in (-1, 0, 1)
    for dz in (-1, 0, 1)
    if abs(dx) + abs(dy) + abs(dz) == 2
)
ROUTES = FACES + EDGES


def slope(m2, m1, p1, p2):
    return (8.0 * (p1 - m1) - (p2 - m2)) * (1.0 / 12.0)


def step_kernel(
    shifts_ref, source_ref, moved_ref, filled_ref, out_ref, start_ref, gathered, column, box, zhalo, acc, slopes, ysend, yrecv, csend, crecv, zsend, zcore, zx, zy,
    send_sem, recv_sem, own_send, own_recv, far_send, far_recv, on_send, on_recv, y_send, y_recv,
    late_send, late_recv, slab_send, slab_recv,
):
    fields = start_ref.shape[0]
    portion = fields // PORTIONS
    groups = zsend.shape[2]
    counts = tuple(lax.axis_size(name) for name in ("gx", "gy", "gz"))
    place = tuple(lax.axis_index(name) for name in ("gx", "gy", "gz"))
    lane = lax.broadcasted_iota(jnp.int32, (8, 128), 1)
    row = lax.broadcasted_iota(jnp.int32, (8, 128), 0)
    zero = jnp.zeros((8, 128), jnp.float32)

    def present(route):
        ok = None
        for d in range(3):
            if route[d] != 0:
                here = place[d] > 0 if route[d] < 0 else place[d] < counts[d] - 1
                ok = here if ok is None else jnp.logical_and(ok, here)
        return ok

    def peer(route):
        return tuple(place[d] + route[d] for d in range(3))

    def opposite(route):
        return tuple(-side for side in route)

    def wipe_field(f, carry):
        for slot in range(2):
            for x in range(14):
                for y in (0, 16) if 3 <= x < 11 else (0, 8, 16):
                    box[slot, f, x, pl.ds(y, 8), :] = zero
        return carry

    lax.fori_loop(0, fields, wipe_field, 0)

    @pl.when(place[1] == counts[1] - 1)
    def _():
        def wipe_column(f, carry):
            for x in range(8):
                column[f, x, pl.ds(8, 8), :] = zero
            return carry

        lax.fori_loop(0, fields, wipe_column, 0)

    def keep_own(f, carry):
        for x in range(8):
            gathered[0, f, x] = filled_ref[f, x]
            column[f, x, pl.ds(0, 8), :] = moved_ref[f, x]
        return carry

    for slot in range(2):
        for z in range(2):
            for g in range(groups):
                zcore[slot, z, g] = zero
            for side in range(2):
                for g in range(2):
                    zx[slot, side, z, g] = zero
                    zy[slot, side, z, g] = zero
            for side in range(2):
                for f in range(MIXED):
                    crecv[slot, z, side, f] = zero

    def wipe_y(f, carry):
        for slot in range(2):
            for side in range(2):
                for j in range(3):
                    for g in range(fields // 8):
                        yrecv[slot, side, f, j, pl.ds(8 * g, 8), :] = zero
        return carry

    lax.fori_loop(0, 8, wipe_y, 0)

    barrier = pltpu.get_barrier_semaphore()
    partner = (place[0] + 1 - 2 * lax.rem(place[0], 2), place[1], place[2])
    across = (lax.rem(place[0] + 2, 4), place[1], place[2])
    total = jnp.int32(2)
    for other in (partner, across):
        pl.semaphore_signal(barrier, inc=1, device_id=other, device_id_type=MESH)
    for route in ROUTES:
        ok = present(route)
        total = total + ok.astype(jnp.int32)

        @pl.when(ok)
        def _(route=route):
            pl.semaphore_signal(barrier, inc=1, device_id=peer(route), device_id_type=MESH)

    pl.semaphore_wait(barrier, total)

    def remote(source, target, sent, got, device):
        return pltpu.make_async_remote_copy(
            src_ref=source,
            dst_ref=target,
            send_sem=sent,
            recv_sem=got,
            device_id=device,
            device_id_type=MESH,
        )

    def far_copy(k):
        part = pl.ds(k * portion, portion)
        return remote(
            filled_ref.at[part], gathered.at[2, part], far_send.at[k], far_recv.at[k], across
        )

    def on_copy(k):
        part = pl.ds(k * portion, portion)
        return remote(
            gathered.at[2, part], gathered.at[3, part], on_send.at[k], on_recv.at[k], partner
        )

    own_copy = remote(filled_ref, gathered.at[1], own_send, own_recv, partner)
    y_copy = remote(
        moved_ref,
        column.at[:, :, pl.ds(8, 8), :],
        y_send,
        y_recv,
        (place[0], place[1] - 1, place[2]),
    )

    @pl.when(place[1] > 0)
    def _():
        y_copy.start()

    for k in range(PORTIONS):
        far_copy(k).start()
    own_copy.start()
    lax.fori_loop(0, fields, keep_own, 0)
    for k in range(PORTIONS):
        far_copy(k).wait_recv()
        on_copy(k).start()
    own_copy.wait()
    for k in range(PORTIONS):
        on_copy(k).wait()
        far_copy(k).wait_send()

    @pl.when(place[1] > 0)
    def _():
        y_copy.wait_send()

    @pl.when(place[1] < counts[1] - 1)
    def _():
        y_copy.wait_recv()

    chosen = source_ref[0]
    shift_y = shifts_ref[1]
    row_spot = row + (place[1] * 8 + shifts_ref[1])
    column_entering = row_spot >= 8 * counts[1]
    for f in range(fields):
        for x in range(8):
            x_spot = jnp.zeros((8, 128), jnp.int32) + (place[0] * 8 + x + shifts_ref[0])
            entering = jnp.logical_or(column_entering, x_spot >= 8 * counts[0])
            name = ORDER[f]
            value = jnp.where(entering, gathered[chosen, name, x], column[name, x, pl.ds(shift_y, 8), :])
            start_ref[name, x] = value
            acc[name, x] = value
            box[0, f, 3 + x, pl.ds(8, 8), :] = value

    def message(number, slot, piece=0):
        route = ROUTES[number]
        sent, got = send_sem.at[number], recv_sem.at[slot, number]
        dx, dy, dz = route
        low = lambda side: 1 if side < 0 else 0
        high = lambda side: 0 if side < 0 else 1
        if dx != 0 and dy == 0 and dz == 0:
            first, late = (0, 2) if dx < 0 else (5, 7)
            start, size = (late, 1) if piece == 1 else (first, 2)
            source = box.at[slot, :, pl.ds(start + 3, size), pl.ds(8, 8), :]
            target = box.at[slot, :, pl.ds(start + (11 if dx < 0 else -5), size), pl.ds(8, 8), :]
            if piece == 1:
                sent, got = late_send.at[high(dx)], late_recv.at[slot, high(dx)]
        elif dy != 0 and dx == 0 and dz == 0:
            source = ysend.at[slot, high(dy), piece]
            target = yrecv.at[slot, low(dy), piece]
            sent, got = slab_send.at[high(dy), piece], slab_recv.at[slot, high(dy), piece]
        elif dz != 0 and dx == 0 and dy == 0:
            source = zsend.at[slot, high(dz)]
            target = zcore.at[slot, low(dz)]
        elif dz == 0:
            source = csend.at[slot, high(dy)]
            target = crecv.at[slot, low(dy), low(dx)]
        elif dy == 0:
            source = zsend.at[slot, high(dz), pl.ds(0, 2)]
            target = zx.at[slot, low(dx), low(dz)]
        else:
            source = zsend.at[slot, high(dz), pl.ds(0, 2)]
            target = zy.at[slot, low(dy), low(dz)]
        return remote(source, target, sent, got, peer(route))

    def launch(slot, wanted, piece=0):
        for number, route in enumerate(ROUTES):
            if wanted(route):

                @pl.when(present(route))
                def _(number=number):
                    message(number, slot, piece).start()

    def is_x(route):
        return route[1] == 0 and route[2] == 0

    def is_y(route):
        return route[0] == 0 and route[2] == 0

    def finish_all(slot, direction):
        for number, route in enumerate(ROUTES):
            ok = present(route if direction == 0 else opposite(route))

            @pl.when(ok)
            def _(number=number, route=route):
                def settle(piece):
                    if direction == 0:
                        message(number, slot, piece).wait_send()
                    else:
                        message(number, slot, piece).wait_recv()

                if is_y(route):
                    lax.fori_loop(0, 8, lambda x, c: (settle(x), c)[1], 0)
                else:
                    settle(0)
                    if is_x(route):
                        settle(1)

    def send_slab(slot, x):
        for side in range(2):
            for j in range(3):
                ysend[slot, side, x, j] = box[slot, :, 3 + x, 8 + 5 * side + j, :]
        launch(slot, is_y, x)

        @pl.when(x == 1)
        def _():
            launch(slot, lambda r: is_x(r) and r[0] < 0)

        @pl.when(x == 6)
        def _():
            launch(slot, lambda r: is_x(r) and r[0] > 0)

        @pl.when(x == 7)
        def _():
            launch(slot, is_x, 1)

    def unpacked(from_low, from_high, t):
        return jnp.where(
            lane < 64,
            pltpu.roll(from_high, (128 - 4 * t) % 128, axis=1),
            pltpu.roll(from_low, (124 - 4 * t) % 128, axis=1),
        )

    def stage(s, carry):
        slot = lax.rem(s, 2)

        for side in range(2):
            for j in range(2):
                first = 8 if side == 0 else 14
                for x in (0, 1, 6, 7):
                    for f in range(MIXED):
                        csend[slot, side, f, pl.ds((x + 4 * j) % 8, 1), :] = box[
                            slot, f, 3 + x, pl.ds(first + j, 1), :
                        ]
        launch(slot, lambda r: r[2] == 0 and r[0] != 0 and r[1] != 0)

        def pack_z(g, c):
            low = zero
            high = zero
            for q in range(4):
                for x in range(8):
                    t = q * 8 + x
                    value = box[slot, 4 * g + q, 3 + x, pl.ds(8, 8), :]
                    inside = jnp.logical_and(lane >= 4 * t, lane < 4 * t + 4)
                    low = jnp.where(inside, pltpu.roll(value, 4 * t, axis=1), low)
                    high = jnp.where(inside, pltpu.roll(value, (4 * t + 4) % 128, axis=1), high)
            zsend[slot, 0, g] = low
            zsend[slot, 1, g] = high
            return c

        lax.fori_loop(0, groups, pack_z, 0)
        launch(slot, lambda r: r[2] != 0)

        finish_all(slot, 1)
        finish_all(slot, 0)

        def spread_y(x, c):
            for j in range(3):
                box[slot, :, 3 + x, 5 + j, :] = yrecv[slot, 0, x, j]
                box[slot, :, 3 + x, 16 + j, :] = yrecv[slot, 1, x, j]
            return c

        lax.fori_loop(0, 8, spread_y, 0)
        for f in range(MIXED):
            for side, first_row in ((0, 6), (1, 16)):
                for j in range(2):
                    box[slot, f, pl.ds(1, 2), first_row + j, :] = crecv[
                        slot, side, 0, f, pl.ds(6 if j == 0 else 2, 2), :
                    ]
                    box[slot, f, pl.ds(11, 2), first_row + j, :] = crecv[
                        slot, side, 1, f, pl.ds(0 if j == 0 else 4, 2), :
                    ]

        def spread_z(g, c):
            from_low = zcore[slot, 0, g]
            from_high = zcore[slot, 1, g]
            for q in range(4):
                for x in range(8):
                    zhalo[4 * g + q, 2 + x, pl.ds(8, 8), :] = unpacked(
                        from_low, from_high, q * 8 + x
                    )
            return c

        lax.fori_loop(0, groups, spread_z, 0)
        for f in range(MIXED):
            g, q = f // 4, f % 4
            for side in range(2):
                low_x, high_x = zx[slot, side, 0, g], zx[slot, side, 1, g]
                for k in range(2):
                    x = 6 + k if side == 0 else k
                    at = k if side == 0 else 10 + k
                    zhalo[f, at, pl.ds(8, 8), :] = unpacked(low_x, high_x, q * 8 + x)
                low_y, high_y = zy[slot, side, 0, g], zy[slot, side, 1, g]
                for x in range(8):
                    zhalo[f, 2 + x, pl.ds(16 * side, 8), :] = unpacked(low_y, high_y, q * 8 + x)

        share = jnp.where(jnp.logical_or(s == 0, s == 3), STEP / 6.0, STEP / 3.0)
        share = share.astype(jnp.float32)
        reach = jnp.where(s == 2, STEP, 0.5 * STEP).astype(jnp.float32)
        later = 1 - slot

        def slab(x, c):
            def at_z(value, halo, amount):
                if amount > 0:
                    return pltpu.roll(jnp.where(lane < amount, halo, value), 128 - amount, axis=1)
                return pltpu.roll(
                    jnp.where(lane >= 128 + amount, halo, value), -amount, axis=1
                )

            def tile(f, dx=0, dy=0):
                return box[slot, f, 3 + x + dx, pl.ds(8 + dy, 8), :]

            def slope_z(value, halo):
                return slope(*(at_z(value, halo, amount) for amount in (-2, -1, 1, 2)))

            def study(name, gradient=False):
                f = PLACE[name]
                centre = tile(f)
                halo = zhalo[f, 2 + x, pl.ds(8, 8), :]
                pairs = []
                grads = []
                for d in range(3):
                    cells = {}
                    for amount in (-3, -2, -1, 1, 2, 3):
                        if d == 0:
                            cells[amount] = tile(f, amount, 0)
                        elif d == 1:
                            cells[amount] = tile(f, 0, amount)
                        else:
                            cells[amount] = at_z(centre, halo, amount)
                    pairs.append([cells[k] + cells[-k] for k in (1, 2, 3)])
                    if gradient:
                        grads.append(slope(cells[-2], cells[-1], cells[1], cells[2]))
                ones, twos, threes = [pairs[0][k] + pairs[1][k] + pairs[2][k] for k in range(3)]
                damp = (threes - 6.0 * twos + 15.0 * ones - 60.0 * centre) * (SIGMA / 64.0)
                lap = (16.0 * ones - twos - 90.0 * centre) * (1.0 / 12.0)
                curves = [
                    (16.0 * pairs[d][0] - pairs[d][1] - 30.0 * centre) * (1.0 / 12.0)
                    for d in range(3)
                ]
                return centre, damp, lap, curves, grads

            def finish(name, rate):
                f = PLACE[name]
                total = acc[name, x] + share * rate
                acc[name, x] = total
                box[later, f, 3 + x, pl.ds(8, 8), :] = start_ref[name, x] + reach * rate

            def across_x(name, y):
                f = PLACE[name]
                return slope(
                    *(box[slot, f, 3 + x + k, pl.ds(y, 8), :] for k in (-2, -1, 1, 2))
                )

            def halo_x(name):
                f = PLACE[name]
                return slope(
                    *(zhalo[f, 2 + x + k, pl.ds(8, 8), :] for k in (-2, -1, 1, 2))
                )

            def along_y(name):
                f = PLACE[name]
                return slope(*(tile(f, 0, k) for k in (-2, -1, 1, 2)))

            def halo_y(name):
                f = PLACE[name]
                return slope(
                    *(zhalo[f, 2 + x, pl.ds(8 + k, 8), :] for k in (-2, -1, 1, 2))
                )

            def mixed_xy(number, value):
                for y in (0, 8, 16):
                    slopes[number, pl.ds(y, 8), :] = value(lambda name: across_x(name, y))
                return slope(*(slopes[number, pl.ds(8 + k, 8), :] for k in (-2, -1, 1, 2)))

            def mixed_xz(value):
                return slope_z(value(lambda name: across_x(name, 8)), value(halo_x))

            def mixed_yz(value):
                return slope_z(value(along_y), value(halo_y))

            both = lambda part: part(17) + 2.0 * part(0)
            only = lambda name: (lambda part: part(name))

            curv, curv_damp, _, _, curv_grad = study(7, True)
            phi, phi_damp, _, phi_curves, _ = study(0)
            lapse, lapse_damp, lapse_lap, lapse_curves, _ = study(17)
            finish(17, lapse_damp - 2.0 * curv)
            finish(7, curv_damp - lapse_lap)
            shift_parts = [study(18 + i, True) for i in range(3)]
            shift_grad = [[shift_parts[j][4][d] for j in range(3)] for d in range(3)]
            spread = shift_grad[0][0] + shift_grad[1][1] + shift_grad[2][2]
            finish(0, phi_damp + (spread - curv) * (1.0 / 6.0))
            crossed = (
                mixed_xy(0, only(19)) + mixed_xz(only(20)),
                mixed_xy(1, only(18)) + mixed_yz(only(20)),
                mixed_xz(only(18)) + mixed_yz(only(19)),
            )
            gamma_grad = []
            gamma_parts = [study(14 + i, True) for i in range(3)]
            gamma_grad = [[gamma_parts[j][4][d] for j in range(3)] for d in range(3)]
            for i in range(3):
                rate = (
                    shift_parts[i][2]
                    - (4.0 / 3.0) * curv_grad[i]
                    + (shift_parts[i][3][i] + crossed[i]) * (1.0 / 3.0)
                )
                finish(14 + i, rate + gamma_parts[i][1])
                driver, driver_damp, _, _, _ = study(21 + i)
                finish(18 + i, shift_parts[i][1] + 0.75 * driver)
                finish(21 + i, driver_damp + rate - DRIVER_DAMP * driver)
            hessian = {
                (0, 1): mixed_xy(2, both),
                (0, 2): mixed_xz(both),
                (1, 2): mixed_yz(both),
            }
            for i in range(3):
                hessian[(i, i)] = lapse_curves[i] + 2.0 * phi_curves[i]
            ricci = []
            free_damp = []
            for n, (i, j) in enumerate(PAIRS):
                free, damp, _, _, _ = study(8 + n)
                free_damp.append(damp)
                _, metric_damp, metric_lap, _, _ = study(1 + n)
                value = shift_grad[i][j] + shift_grad[j][i] - 2.0 * free
                if i == j:
                    value = value - (2.0 / 3.0) * spread
                finish(1 + n, value + metric_damp)
                ricci.append(
                    0.5 * (gamma_grad[i][j] + gamma_grad[j][i] - metric_lap) - hessian[(i, j)]
                )
            trace = (ricci[0] + ricci[3] + ricci[5]) * (1.0 / 3.0)
            for n, (i, j) in enumerate(PAIRS):
                value = ricci[n] - trace if i == j else ricci[n]
                finish(8 + n, value + free_damp[n])

            @pl.when(s < 3)
            def _():
                send_slab(later, x)

            return c

        lax.fori_loop(0, 8, slab, 0)
        return carry

    def first_slab(x, carry):
        send_slab(0, x)
        return carry

    lax.fori_loop(0, 8, first_slab, 0)
    lax.fori_loop(0, 4, stage, 0)

    def hand_out(f, carry):
        for x in range(8):
            out_ref[f, x] = acc[f, x]
        return carry

    lax.fori_loop(0, fields, hand_out, 0)


def advance(shifts, source, moved, filled):
    fields, width, height, depth = moved.shape
    groups = fields * width // 32
    tall = height + 16

    def buffer(*sizes):
        return pltpu.VMEM(sizes + (depth,), jnp.float32)

    return pl.pallas_call(
        step_kernel,
        out_shape=jax.ShapeDtypeStruct(moved.shape, jnp.float32),
        in_specs=[pl.BlockSpec(memory_space=pltpu.SMEM)] * 2
        + [pl.BlockSpec(memory_space=pltpu.VMEM)] * 2,
        out_specs=pl.BlockSpec(memory_space=pltpu.VMEM),
        scratch_shapes=[
            buffer(fields, width, height),
            buffer(4, fields, width, height),
            buffer(fields, width, 2 * height),
            buffer(2, fields, width + 6, tall),
            buffer(fields, width + 4, tall),
            buffer(fields, width, height),
            buffer(3, tall),
            buffer(2, 2, width, 3, fields),
            buffer(2, 2, width, 3, fields),
            buffer(2, 2, MIXED, width),
            buffer(2, 2, 2, MIXED, width),
            buffer(2, 2, groups, height),
            buffer(2, 2, groups, height),
            buffer(2, 2, 2, 2, height),
            buffer(2, 2, 2, 2, height),
            pltpu.SemaphoreType.DMA((len(ROUTES),)),
            pltpu.SemaphoreType.DMA((2, len(ROUTES))),
            pltpu.SemaphoreType.DMA,
            pltpu.SemaphoreType.DMA,
            pltpu.SemaphoreType.DMA((PORTIONS,)),
            pltpu.SemaphoreType.DMA((PORTIONS,)),
            pltpu.SemaphoreType.DMA((PORTIONS,)),
            pltpu.SemaphoreType.DMA((PORTIONS,)),
            pltpu.SemaphoreType.DMA,
            pltpu.SemaphoreType.DMA,
            pltpu.SemaphoreType.DMA((2,)),
            pltpu.SemaphoreType.DMA((2, 2)),
            pltpu.SemaphoreType.DMA((2, width)),
            pltpu.SemaphoreType.DMA((2, 2, width)),
        ],
        compiler_params=pltpu.CompilerParams(
            collective_id=0, has_side_effects=True, vmem_limit_bytes=48 * 1024 * 1024
        ),
    )(shifts, source, moved, filled)


def lagrange(shift, rows, cols):
    matrix = np.zeros((rows, cols), np.float32)
    for line in range(rows):
        spot = line + shift
        first = spot // 2 + spot % 2
        for t, weight in enumerate(ODD_W if spot % 2 else EVEN_W):
            if first + t < cols:
                matrix[line, first + t] = weight
    return matrix


def lagrange_at(shift, rows, cols):
    table = np.stack([lagrange(s, rows, cols) for s in range(rows + 1)])
    return lax.dynamic_index_in_dim(jnp.asarray(table), shift, 0, keepdims=False)


def body(state, coarse_bricks, shifts, brick_owner):
    fields, width, height, depth = state.shape
    brick_side = width + 4
    brick_depth = depth // 2 + 4
    shift_x = shifts[0]
    shift_y = shifts[1]
    beyond_x = passed_along(state, "gx", -1)
    moved = lax.dynamic_slice_in_dim(
        jnp.concatenate([state, beyond_x], axis=1), shift_x, width, axis=1
    )
    place_x = lax.axis_index("gx")
    wanted = jnp.sum(
        jnp.where(jnp.arange(brick_owner.shape[0], dtype=jnp.int32) == place_x, brick_owner, 0)
    )
    brick = coarse_bricks.reshape((fields, brick_side, brick_side, brick_depth))
    along_x = lagrange_at(shift_x, width, brick_side)
    along_y = lagrange_at(shift_y, height, brick_side)
    along_z = jnp.asarray(lagrange(0, depth, brick_depth))
    first_pass = jnp.einsum("fpqr,kr->fpqk", brick, along_z, precision=HIGH)
    second_pass = jnp.einsum("fpqk,jq->fpjk", first_pass, along_y, precision=HIGH)
    filled = jnp.einsum("fpjk,ip->fijk", second_pass, along_x, precision=HIGH)
    source = jnp.bitwise_xor(wanted, place_x).astype(jnp.int32).reshape(1)
    return advance(shifts, source, moved, filled)


def solution(mesh):
    return jax.shard_map(
        body,
        mesh=mesh,
        in_specs=(P(None, "gx", "gy", "gz"), P("gx", "gy", "gz", None), P(), P()),
        out_specs=P(None, "gx", "gy", "gz"),
        check_vma=False,
    )
```

```python
import jax
import jax.numpy as jnp
import numpy as np
from jax import lax
from jax.experimental import pallas as pl
from jax.experimental.pallas import tpu as pltpu
from jax.sharding import PartitionSpec as P

EVEN_W = (-0.0390625, 0.2734375, 0.8203125, -0.0546875)
ODD_W = (-0.0546875, 0.8203125, 0.2734375, -0.0390625)
PAIRS = ((0, 0), (0, 1), (0, 2), (1, 1), (1, 2), (2, 2))
SIGMA = 0.3
DRIVER_DAMP = 2.0
STEP = 0.25
HIGH = lax.Precision.HIGHEST


def passed_along(block, axis, distance):
    devices = range(lax.axis_size(axis))
    route = [(i - distance, i) for i in devices if i - distance in devices]
    return lax.ppermute(block, axis, route)


MESH = pl.DeviceIdType.MESH
ORDER = (0, 17, 18, 19, 20, 1, 2, 3, 4, 5, 6, 7, 8, 9, 10, 11, 12, 13, 14, 15, 16, 21, 22, 23)
PLACE = {field: place for place, field in enumerate(ORDER)}
MIXED = 5
PORTIONS = 8
FACES = tuple(
    tuple(side if d == axis else 0 for d in range(3)) for axis in range(3) for side in (-1, 1)
)
EDGES = tuple(
    (dx, dy, dz)
    for dx in (-1, 0, 1)
    for dy in (-1, 0, 1)
    for dz in (-1, 0, 1)
    if abs(dx) + abs(dy) + abs(dz) == 2
)
ROUTES = FACES + EDGES


def slope(m2, m1, p1, p2):
    return (8.0 * (p1 - m1) - (p2 - m2)) * (1.0 / 12.0)


def step_kernel(
    shifts_ref, source_ref, moved_ref, filled_ref, out_ref, start_ref, gathered, column, pair, box, zhalo, acc, slopes, ysend, yrecv, csend, crecv, zsend, zcore, zx, zy,
    send_sem, recv_sem, own_send, own_recv, far_send, far_recv, on_send, on_recv, y_send, y_recv,
    late_send, late_recv, slab_send, slab_recv,
):
    fields = start_ref.shape[0]
    groups = zsend.shape[2]
    counts = tuple(lax.axis_size(name) for name in ("gx", "gy", "gz"))
    place = tuple(lax.axis_index(name) for name in ("gx", "gy", "gz"))
    lane = lax.broadcasted_iota(jnp.int32, (8, 128), 1)
    row = lax.broadcasted_iota(jnp.int32, (8, 128), 0)
    zero = jnp.zeros((8, 128), jnp.float32)

    def present(route):
        ok = None
        for d in range(3):
            if route[d] != 0:
                here = place[d] > 0 if route[d] < 0 else place[d] < counts[d] - 1
                ok = here if ok is None else jnp.logical_and(ok, here)
        return ok

    def peer(route):
        return tuple(place[d] + route[d] for d in range(3))

    def opposite(route):
        return tuple(-side for side in route)

    def wipe_field(f, carry):
        for slot in range(2):
            for x in range(14):
                for y in (0, 16) if 3 <= x < 11 else (0, 8, 16):
                    box[slot, f, x, pl.ds(y, 8), :] = zero
        return carry

    lax.fori_loop(0, fields, wipe_field, 0)

    @pl.when(place[1] == counts[1] - 1)
    def _():
        def wipe_column(f, carry):
            for x in range(8):
                column[f, x, pl.ds(8, 8), :] = zero
            return carry

        lax.fori_loop(0, fields, wipe_column, 0)

    def keep_own(f, carry):
        for x in range(8):
            gathered[0, f, x] = filled_ref[f, x]
            column[f, x, pl.ds(0, 8), :] = moved_ref[f, x]
        return carry

    for slot in range(2):
        for z in range(2):
            for g in range(groups):
                zcore[slot, z, g] = zero
            for side in range(2):
                for g in range(2):
                    zx[slot, side, z, g] = zero
                    zy[slot, side, z, g] = zero
            for side in range(2):
                for f in range(MIXED):
                    crecv[slot, z, side, f] = zero

    def wipe_y(f, carry):
        for slot in range(2):
            for side in range(2):
                for j in range(3):
                    for g in range(fields // 8):
                        yrecv[slot, side, f, j, pl.ds(8 * g, 8), :] = zero
        return carry

    lax.fori_loop(0, 8, wipe_y, 0)

    barrier = pltpu.get_barrier_semaphore()
    partner = (place[0] + 1 - 2 * lax.rem(place[0], 2), place[1], place[2])
    across = (lax.rem(place[0] + 2, 4), place[1], place[2])
    total = jnp.int32(2)
    for other in (partner, across):
        pl.semaphore_signal(barrier, inc=1, device_id=other, device_id_type=MESH)
    for route in ROUTES:
        ok = present(route)
        total = total + ok.astype(jnp.int32)

        @pl.when(ok)
        def _(route=route):
            pl.semaphore_signal(barrier, inc=1, device_id=peer(route), device_id_type=MESH)

    pl.semaphore_wait(barrier, total)

    def remote(source, target, sent, got, device):
        return pltpu.make_async_remote_copy(
            src_ref=source,
            dst_ref=target,
            send_sem=sent,
            recv_sem=got,
            device_id=device,
            device_id_type=MESH,
        )

    def far_copy(k):
        part = pl.ds(k, 1)
        return remote(
            filled_ref.at[:, part], gathered.at[2, :, part], far_send.at[k], far_recv.at[k], across
        )

    def on_copy(k):
        part = pl.ds(k, 1)
        return remote(
            gathered.at[2, :, part], gathered.at[3, :, part], on_send.at[k], on_recv.at[k], partner
        )

    own_copy = remote(filled_ref, gathered.at[1], own_send, own_recv, partner)
    def y_copy(k):
        return remote(
            moved_ref.at[:, pl.ds(k, 1)],
            column.at[:, pl.ds(k, 1), pl.ds(8, 8), :],
            y_send.at[k],
            y_recv.at[k],
            (place[0], place[1] - 1, place[2]),
        )

    @pl.when(place[1] > 0)
    def _():
        for k in range(PORTIONS):
            y_copy(k).start()

    for k in range(PORTIONS):
        far_copy(k).start()
    own_copy.start()
    lax.fori_loop(0, fields, keep_own, 0)
    own_copy.wait()
    picked = jnp.zeros((8, 128), jnp.int32) + source_ref[0]
    shift_y = shifts_ref[1]
    row_spot = row + (place[1] * 8 + shifts_ref[1])
    column_entering = row_spot >= 8 * counts[1]

    def message(number, slot, piece=0):
        route = ROUTES[number]
        sent, got = send_sem.at[number], recv_sem.at[slot, number]
        dx, dy, dz = route
        low = lambda side: 1 if side < 0 else 0
        high = lambda side: 0 if side < 0 else 1
        if dx != 0 and dy == 0 and dz == 0:
            first, late = (0, 2) if dx < 0 else (5, 7)
            start, size = (late, 1) if piece == 1 else (first, 2)
            source = box.at[slot, :, pl.ds(start + 3, size), pl.ds(8, 8), :]
            target = box.at[slot, :, pl.ds(start + (11 if dx < 0 else -5), size), pl.ds(8, 8), :]
            if piece == 1:
                sent, got = late_send.at[high(dx)], late_recv.at[slot, high(dx)]
        elif dy != 0 and dx == 0 and dz == 0:
            source = ysend.at[slot, high(dy), piece]
            target = yrecv.at[slot, low(dy), piece]
            sent, got = slab_send.at[high(dy), piece], slab_recv.at[slot, high(dy), piece]
        elif dz != 0 and dx == 0 and dy == 0:
            source = zsend.at[slot, high(dz)]
            target = zcore.at[slot, low(dz)]
        elif dz == 0:
            source = csend.at[slot, high(dy)]
            target = crecv.at[slot, low(dy), low(dx)]
        elif dy == 0:
            source = zsend.at[slot, high(dz), pl.ds(0, 2)]
            target = zx.at[slot, low(dx), low(dz)]
        else:
            source = zsend.at[slot, high(dz), pl.ds(0, 2)]
            target = zy.at[slot, low(dy), low(dz)]
        return remote(source, target, sent, got, peer(route))

    def launch(slot, wanted, piece=0):
        for number, route in enumerate(ROUTES):
            if wanted(route):

                @pl.when(present(route))
                def _(number=number):
                    message(number, slot, piece).start()

    def is_x(route):
        return route[1] == 0 and route[2] == 0

    def is_y(route):
        return route[0] == 0 and route[2] == 0

    def finish_all(slot, direction):
        for number, route in enumerate(ROUTES):
            ok = present(route if direction == 0 else opposite(route))

            @pl.when(ok)
            def _(number=number, route=route):
                def settle(piece):
                    if direction == 0:
                        message(number, slot, piece).wait_send()
                    else:
                        message(number, slot, piece).wait_recv()

                if is_y(route):
                    lax.fori_loop(0, 8, lambda x, c: (settle(x), c)[1], 0)
                else:
                    settle(0)
                    if is_x(route):
                        settle(1)

    def send_slab(slot, x):
        for side in range(2):
            for j in range(3):
                ysend[slot, side, x, j] = box[slot, :, 3 + x, 8 + 5 * side + j, :]
        launch(slot, is_y, x)

        @pl.when(x == 1)
        def _():
            launch(slot, lambda r: is_x(r) and r[0] < 0)

        @pl.when(x == 6)
        def _():
            launch(slot, lambda r: is_x(r) and r[0] > 0)

        @pl.when(x == 7)
        def _():
            launch(slot, is_x, 1)

    def unpacked(from_low, from_high, t):
        return jnp.where(
            lane < 64,
            pltpu.roll(from_high, (128 - 4 * t) % 128, axis=1),
            pltpu.roll(from_low, (124 - 4 * t) % 128, axis=1),
        )

    def stage(s, carry):
        slot = lax.rem(s, 2)

        for side in range(2):
            for j in range(2):
                first = 8 if side == 0 else 14
                for x in (0, 1, 6, 7):
                    for f in range(MIXED):
                        csend[slot, side, f, pl.ds((x + 4 * j) % 8, 1), :] = box[
                            slot, f, 3 + x, pl.ds(first + j, 1), :
                        ]
        launch(slot, lambda r: r[2] == 0 and r[0] != 0 and r[1] != 0)

        def pack_z(g, c):
            low = zero
            high = zero
            for q in range(4):
                for x in range(8):
                    t = q * 8 + x
                    value = box[slot, 4 * g + q, 3 + x, pl.ds(8, 8), :]
                    inside = jnp.logical_and(lane >= 4 * t, lane < 4 * t + 4)
                    low = jnp.where(inside, pltpu.roll(value, 4 * t, axis=1), low)
                    high = jnp.where(inside, pltpu.roll(value, (4 * t + 4) % 128, axis=1), high)
            zsend[slot, 0, g] = low
            zsend[slot, 1, g] = high
            return c

        lax.fori_loop(0, groups, pack_z, 0)
        launch(slot, lambda r: r[2] != 0)

        finish_all(slot, 1)
        finish_all(slot, 0)

        def spread_y(x, c):
            for j in range(3):
                box[slot, :, 3 + x, 5 + j, :] = yrecv[slot, 0, x, j]
                box[slot, :, 3 + x, 16 + j, :] = yrecv[slot, 1, x, j]
            return c

        lax.fori_loop(0, 8, spread_y, 0)
        for f in range(MIXED):
            for side, first_row in ((0, 6), (1, 16)):
                for j in range(2):
                    box[slot, f, pl.ds(1, 2), first_row + j, :] = crecv[
                        slot, side, 0, f, pl.ds(6 if j == 0 else 2, 2), :
                    ]
                    box[slot, f, pl.ds(11, 2), first_row + j, :] = crecv[
                        slot, side, 1, f, pl.ds(0 if j == 0 else 4, 2), :
                    ]

        def spread_z(g, c):
            from_low = zcore[slot, 0, g]
            from_high = zcore[slot, 1, g]
            for q in range(4):
                for x in range(8):
                    zhalo[4 * g + q, 2 + x, pl.ds(8, 8), :] = unpacked(
                        from_low, from_high, q * 8 + x
                    )
            return c

        lax.fori_loop(0, groups, spread_z, 0)
        for f in range(MIXED):
            g, q = f // 4, f % 4
            for side in range(2):
                low_x, high_x = zx[slot, side, 0, g], zx[slot, side, 1, g]
                for k in range(2):
                    x = 6 + k if side == 0 else k
                    at = k if side == 0 else 10 + k
                    zhalo[f, at, pl.ds(8, 8), :] = unpacked(low_x, high_x, q * 8 + x)
                low_y, high_y = zy[slot, side, 0, g], zy[slot, side, 1, g]
                for x in range(8):
                    zhalo[f, 2 + x, pl.ds(16 * side, 8), :] = unpacked(low_y, high_y, q * 8 + x)

        share = jnp.where(jnp.logical_or(s == 0, s == 3), STEP / 6.0, STEP / 3.0)
        share = share.astype(jnp.float32)
        reach = jnp.where(s == 2, STEP, 0.5 * STEP).astype(jnp.float32)
        later = 1 - slot

        def slab(x, c):
            def at_z(value, halo, amount):
                if amount > 0:
                    return pltpu.roll(jnp.where(lane < amount, halo, value), 128 - amount, axis=1)
                return pltpu.roll(
                    jnp.where(lane >= 128 + amount, halo, value), -amount, axis=1
                )

            def tile(f, dx=0, dy=0):
                return box[slot, f, 3 + x + dx, pl.ds(8 + dy, 8), :]

            def slope_z(value, halo):
                return slope(*(at_z(value, halo, amount) for amount in (-2, -1, 1, 2)))

            def study(name, gradient=False):
                f = PLACE[name]
                centre = tile(f)
                halo = zhalo[f, 2 + x, pl.ds(8, 8), :]
                pairs = []
                grads = []
                for d in range(3):
                    cells = {}
                    for amount in (-3, -2, -1, 1, 2, 3):
                        if d == 0:
                            cells[amount] = tile(f, amount, 0)
                        elif d == 1:
                            cells[amount] = tile(f, 0, amount)
                        else:
                            cells[amount] = at_z(centre, halo, amount)
                    pairs.append([cells[k] + cells[-k] for k in (1, 2, 3)])
                    if gradient:
                        grads.append(slope(cells[-2], cells[-1], cells[1], cells[2]))
                ones, twos, threes = [pairs[0][k] + pairs[1][k] + pairs[2][k] for k in range(3)]
                damp = (threes - 6.0 * twos + 15.0 * ones - 60.0 * centre) * (SIGMA / 64.0)
                lap = (16.0 * ones - twos - 90.0 * centre) * (1.0 / 12.0)
                curves = [
                    (16.0 * pairs[d][0] - pairs[d][1] - 30.0 * centre) * (1.0 / 12.0)
                    for d in range(3)
                ]
                return centre, damp, lap, curves, grads

            def finish(name, rate):
                f = PLACE[name]
                total = acc[name, x] + share * rate
                acc[name, x] = total
                box[later, f, 3 + x, pl.ds(8, 8), :] = start_ref[name, x] + reach * rate

            def across_x(name, y):
                f = PLACE[name]
                return slope(
                    *(box[slot, f, 3 + x + k, pl.ds(y, 8), :] for k in (-2, -1, 1, 2))
                )

            def halo_x(name):
                f = PLACE[name]
                return slope(
                    *(zhalo[f, 2 + x + k, pl.ds(8, 8), :] for k in (-2, -1, 1, 2))
                )

            def along_y(name):
                f = PLACE[name]
                return slope(*(tile(f, 0, k) for k in (-2, -1, 1, 2)))

            def halo_y(name):
                f = PLACE[name]
                return slope(
                    *(zhalo[f, 2 + x, pl.ds(8 + k, 8), :] for k in (-2, -1, 1, 2))
                )

            def mixed_xy(number, value):
                for y in (0, 8, 16):
                    slopes[number, pl.ds(y, 8), :] = value(lambda name: across_x(name, y))
                return slope(*(slopes[number, pl.ds(8 + k, 8), :] for k in (-2, -1, 1, 2)))

            def mixed_xz(value):
                return slope_z(value(lambda name: across_x(name, 8)), value(halo_x))

            def mixed_yz(value):
                return slope_z(value(along_y), value(halo_y))

            both = lambda part: part(17) + 2.0 * part(0)
            only = lambda name: (lambda part: part(name))

            curv, curv_damp, _, _, curv_grad = study(7, True)
            phi, phi_damp, _, phi_curves, _ = study(0)
            lapse, lapse_damp, lapse_lap, lapse_curves, _ = study(17)
            finish(17, lapse_damp - 2.0 * curv)
            finish(7, curv_damp - lapse_lap)
            shift_parts = [study(18 + i, True) for i in range(3)]
            shift_grad = [[shift_parts[j][4][d] for j in range(3)] for d in range(3)]
            spread = shift_grad[0][0] + shift_grad[1][1] + shift_grad[2][2]
            finish(0, phi_damp + (spread - curv) * (1.0 / 6.0))
            crossed = (
                mixed_xy(0, only(19)) + mixed_xz(only(20)),
                mixed_xy(1, only(18)) + mixed_yz(only(20)),
                mixed_xz(only(18)) + mixed_yz(only(19)),
            )
            gamma_grad = []
            gamma_parts = [study(14 + i, True) for i in range(3)]
            gamma_grad = [[gamma_parts[j][4][d] for j in range(3)] for d in range(3)]
            for i in range(3):
                rate = (
                    shift_parts[i][2]
                    - (4.0 / 3.0) * curv_grad[i]
                    + (shift_parts[i][3][i] + crossed[i]) * (1.0 / 3.0)
                )
                finish(14 + i, rate + gamma_parts[i][1])
                driver, driver_damp, _, _, _ = study(21 + i)
                finish(18 + i, shift_parts[i][1] + 0.75 * driver)
                finish(21 + i, driver_damp + rate - DRIVER_DAMP * driver)
            hessian = {
                (0, 1): mixed_xy(2, both),
                (0, 2): mixed_xz(both),
                (1, 2): mixed_yz(both),
            }
            for i in range(3):
                hessian[(i, i)] = lapse_curves[i] + 2.0 * phi_curves[i]
            ricci = []
            free_damp = []
            for n, (i, j) in enumerate(PAIRS):
                free, damp, _, _, _ = study(8 + n)
                free_damp.append(damp)
                _, metric_damp, metric_lap, _, _ = study(1 + n)
                value = shift_grad[i][j] + shift_grad[j][i] - 2.0 * free
                if i == j:
                    value = value - (2.0 / 3.0) * spread
                finish(1 + n, value + metric_damp)
                ricci.append(
                    0.5 * (gamma_grad[i][j] + gamma_grad[j][i] - metric_lap) - hessian[(i, j)]
                )
            trace = (ricci[0] + ricci[3] + ricci[5]) * (1.0 / 3.0)
            for n, (i, j) in enumerate(PAIRS):
                value = ricci[n] - trace if i == j else ricci[n]
                finish(8 + n, value + free_damp[n])

            @pl.when(s < 3)
            def _():
                send_slab(later, x)

            return c

        lax.fori_loop(0, 8, slab, 0)
        return carry

    def first_slab(x, carry):
        far_copy(x).wait_recv()
        on_copy(x).start()

        @pl.when(place[1] < counts[1] - 1)
        def _():
            y_copy(x).wait_recv()

        on_copy(x).wait_recv()
        x_spot = jnp.zeros((8, 128), jnp.int32) + (place[0] * 8 + x + shifts_ref[0])
        entering = jnp.logical_or(column_entering, x_spot >= 8 * counts[0])
        for f in range(fields):
            name = ORDER[f]
            refill = gathered[0, name, x]
            for k in range(1, 4):
                refill = jnp.where(picked == k, gathered[k, name, x], refill)
            pair[f, pl.ds(0, 8), :] = column[name, x, pl.ds(0, 8), :]
            pair[f, pl.ds(8, 8), :] = column[name, x, pl.ds(8, 8), :]
            value = jnp.where(entering, refill, pair[f, pl.ds(shift_y, 8), :])
            start_ref[name, x] = value
            acc[name, x] = value
            box[0, f, 3 + x, pl.ds(8, 8), :] = value
        send_slab(0, x)
        return carry

    lax.fori_loop(0, 8, first_slab, 0)

    def settle_sends(x, carry):
        far_copy(x).wait_send()
        on_copy(x).wait_send()

        @pl.when(place[1] > 0)
        def _():
            y_copy(x).wait_send()

        return carry

    lax.fori_loop(0, PORTIONS, settle_sends, 0)
    lax.fori_loop(0, 4, stage, 0)

    def hand_out(f, carry):
        for x in range(8):
            out_ref[f, x] = acc[f, x]
        return carry

    lax.fori_loop(0, fields, hand_out, 0)


def advance(shifts, source, moved, filled):
    fields, width, height, depth = moved.shape
    groups = fields * width // 32
    tall = height + 16

    def buffer(*sizes):
        return pltpu.VMEM(sizes + (depth,), jnp.float32)

    return pl.pallas_call(
        step_kernel,
        out_shape=jax.ShapeDtypeStruct(moved.shape, jnp.float32),
        in_specs=[pl.BlockSpec(memory_space=pltpu.SMEM)] * 2
        + [pl.BlockSpec(memory_space=pltpu.VMEM)] * 2,
        out_specs=pl.BlockSpec(memory_space=pltpu.VMEM),
        scratch_shapes=[
            buffer(fields, width, height),
            buffer(4, fields, width, height),
            buffer(fields, width, 2 * height),
            buffer(fields, 2 * height),
            buffer(2, fields, width + 6, tall),
            buffer(fields, width + 4, tall),
            buffer(fields, width, height),
            buffer(3, tall),
            buffer(2, 2, width, 3, fields),
            buffer(2, 2, width, 3, fields),
            buffer(2, 2, MIXED, width),
            buffer(2, 2, 2, MIXED, width),
            buffer(2, 2, groups, height),
            buffer(2, 2, groups, height),
            buffer(2, 2, 2, 2, height),
            buffer(2, 2, 2, 2, height),
            pltpu.SemaphoreType.DMA((len(ROUTES),)),
            pltpu.SemaphoreType.DMA((2, len(ROUTES))),
            pltpu.SemaphoreType.DMA,
            pltpu.SemaphoreType.DMA,
            pltpu.SemaphoreType.DMA((PORTIONS,)),
            pltpu.SemaphoreType.DMA((PORTIONS,)),
            pltpu.SemaphoreType.DMA((PORTIONS,)),
            pltpu.SemaphoreType.DMA((PORTIONS,)),
            pltpu.SemaphoreType.DMA((PORTIONS,)),
            pltpu.SemaphoreType.DMA((PORTIONS,)),
            pltpu.SemaphoreType.DMA((2,)),
            pltpu.SemaphoreType.DMA((2, 2)),
            pltpu.SemaphoreType.DMA((2, width)),
            pltpu.SemaphoreType.DMA((2, 2, width)),
        ],
        compiler_params=pltpu.CompilerParams(
            collective_id=0, has_side_effects=True, vmem_limit_bytes=48 * 1024 * 1024
        ),
    )(shifts, source, moved, filled)


def lagrange(shift, rows, cols):
    matrix = np.zeros((rows, cols), np.float32)
    for line in range(rows):
        spot = line + shift
        first = spot // 2 + spot % 2
        for t, weight in enumerate(ODD_W if spot % 2 else EVEN_W):
            if first + t < cols:
                matrix[line, first + t] = weight
    return matrix


def lagrange_at(shift, rows, cols):
    table = np.stack([lagrange(s, rows, cols) for s in range(rows + 1)])
    return lax.dynamic_index_in_dim(jnp.asarray(table), shift, 0, keepdims=False)


def body(state, coarse_bricks, shifts, brick_owner):
    fields, width, height, depth = state.shape
    brick_side = width + 4
    brick_depth = depth // 2 + 4
    shift_x = shifts[0]
    shift_y = shifts[1]
    beyond_x = passed_along(state, "gx", -1)
    moved = lax.dynamic_slice_in_dim(
        jnp.concatenate([state, beyond_x], axis=1), shift_x, width, axis=1
    )
    place_x = lax.axis_index("gx")
    wanted = jnp.sum(
        jnp.where(jnp.arange(brick_owner.shape[0], dtype=jnp.int32) == place_x, brick_owner, 0)
    )
    brick = coarse_bricks.reshape((fields, brick_side, brick_side, brick_depth))
    along_x = lagrange_at(shift_x, width, brick_side)
    along_y = lagrange_at(shift_y, height, brick_side)
    along_z = jnp.asarray(lagrange(0, depth, brick_depth))
    first_pass = jnp.einsum("fpqr,kr->fpqk", brick, along_z, precision=HIGH)
    second_pass = jnp.einsum("fpqk,jq->fpjk", first_pass, along_y, precision=HIGH)
    filled = jnp.einsum("fpjk,ip->fijk", second_pass, along_x, precision=HIGH)
    source = jnp.bitwise_xor(wanted, place_x).astype(jnp.int32).reshape(1)
    return advance(shifts, source, moved, filled)


def solution(mesh):
    return jax.shard_map(
        body,
        mesh=mesh,
        in_specs=(P(None, "gx", "gy", "gz"), P("gx", "gy", "gz", None), P(), P()),
        out_specs=P(None, "gx", "gy", "gz"),
        check_vma=False,
    )
```
